512 devices in a mesh: star: 64 (over x, z), pix: 8 (over y, core).
Axes of the slice: x: 4, y: 4, z: 16, core: 2. Of those that a mesh axis runs over, the one named last changes fastest.
Arguments:
- flux: bfloat16 [20480, 8192], P('star', 'pix'), may hold values from -8 to 8
- inv_var: bfloat16 [20480, 8192], P('star', 'pix'), may hold values from 0.099609375 to 10
- coeffs: float32 [231, 8192], P(None, 'pix'), may hold values from -0.375 to 0.375
- labels: float32 [20480, 20], P('star'), may hold values from -4 to 4
Outputs:
- new_coeffs: float32 [231, 8192], P(None, 'pix')
- new_labels: float32 [20480, 20], P('star')
The draws below stay inside these ranges and needn't reach their ends.
All inputs are finite; a program needn't handle non-finite values.
Results may differ from the reference program's by a relative error of at most 0.0087.
Values sent between devices are 32-bit elements; how exact they have to be, the bound alone decides.
A program may use at most 64 MiB of HBM per device.

```python
import math
import jax
import jax.numpy as jnp
import numpy as np
from jax import lax

PIX = 8192
LABELS = 20
FEAT = 231
ALTS = 2
STARS = 20480


def raised(values, key, source, target, parts, factor):
    owner, partner = [(jnp.arange(values.shape[axis_at]) // (values.shape[axis_at] // parts)).reshape([-1 if axis == axis_at else 1 for axis in range(values.ndim)]) for axis_at in (source, target)]
    chosen = jax.random.permutation(key, parts)[partner]
    strong = (owner == chosen) | (owner == (partner + parts // 2) % parts)
    return jnp.where(strong, factor * values, values)


def block_scale(stream_key, extent, cuts, least, high):
    def one(dim, parts):
        heights = jax.random.uniform(jax.random.fold_in(jax.random.fold_in(stream_key, 6), dim), (parts,), jnp.float32, least / len(cuts), high / len(cuts))
        return jnp.repeat(jnp.exp(heights), extent[dim] // parts).reshape((-1,) + (1,) * (len(extent) - dim - 1))

    factor_of = one(*cuts[0])
    for cut in cuts[1:]:
        factor_of = factor_of * one(*cut)
    return factor_of


def centred(stream_key, extent, deviation, bound, cuts=(), kind=jnp.bfloat16):
    gain = block_scale(stream_key, extent, cuts, -0.22, 0.18) if cuts else 1.0
    result = jax.random.normal(stream_key, extent, jnp.float32) * deviation * gain
    return jnp.minimum(jnp.maximum(result, -bound), bound).astype(kind)


def noise_with(own_key, shape, width, bound, pieces, heavy, kind=jnp.bfloat16):
    entries = width * jax.random.normal(own_key, shape, jnp.float32)
    if pieces:
        entries = entries * block_scale(own_key, shape, pieces, -0.22, 0.18)
    return jnp.clip(raised(entries, jax.random.fold_in(own_key, 3), *heavy), -bound, bound).astype(kind)


def setup_inputs(seed: int = 0) -> dict:
    seeds = jax.random.split(jax.random.key(seed), 5)
    return {
        "flux": noise_with(seeds[0], (STARS, PIX), 1.0, 8.0, ((0, 64), (1, 8)), (0, 1, 64, 4.0)),
        "inv_var": jnp.clip(jnp.exp(math.log(10.0) - 4.609084 * jax.random.uniform(seeds[1], (STARS, PIX), jnp.float32) ** block_scale(seeds[1], (STARS, PIX), ((0, 64), (1, 8)), -0.2, 0.2)), 0.099609375, 10.0).astype(jnp.bfloat16),
        "coeffs": centred(seeds[2], (FEAT, PIX), FEAT ** -0.5, 0.375, ((1, 8),), jnp.float32),
        "labels": centred(seeds[3], (STARS, LABELS), 1.0, 4.0, ((0, 64),), jnp.float32),
    }


step_size = 0.25


def pair_tables(count):
    left_index = []
    right_index = []
    for row_index in range(count):
        for col_index in range(row_index, count):
            left_index.append(row_index)
            right_index.append(col_index)
    pair_table = np.zeros((count, count), np.int32)
    doubling = np.ones((count, count), np.float32)
    for position in range(len(left_index)):
        pair_table[left_index[position], right_index[position]] = 1 + count + position
        pair_table[right_index[position], left_index[position]] = 1 + count + position
    for row_index in range(count):
        doubling[row_index, row_index] = 2.0
    return np.array(left_index, np.int32), np.array(right_index, np.int32), pair_table, doubling


def features(labels):
    left_index, right_index, pair_table, doubling = pair_tables(labels.shape[1])
    quad = labels[:, left_index] * labels[:, right_index]
    ones = jnp.ones((labels.shape[0], 1), labels.dtype)
    return jnp.concatenate([ones, labels, quad], axis=1)


def fdot(left, right):
    return jnp.dot(left.astype(jnp.float32), right.astype(jnp.float32))


def reference(flux, inv_var, coeffs, labels):
    count = labels.shape[1]
    left_index, right_index, pair_table, doubling = pair_tables(count)
    flux_f = flux.astype(jnp.float32)
    ivar_f = inv_var.astype(jnp.float32)
    theta = coeffs
    lab = labels
    for turn in range(ALTS):
        feat = features(lab)
        feat_b = feat.astype(jnp.bfloat16)
        lab_b = lab.astype(jnp.bfloat16)
        sq_b = (feat * feat).astype(jnp.bfloat16)
        theta_b = theta.astype(jnp.bfloat16)
        weighted = (ivar_f * (flux_f - fdot(feat_b, theta_b))).astype(jnp.bfloat16)
        grad = fdot(feat_b.T, weighted)
        curv = 1.0 + fdot(sq_b.T, inv_var)
        theta = theta + step_size * grad / curv
        theta_b = theta.astype(jnp.bfloat16)
        rounded = lax.optimization_barrier((ivar_f * (flux_f - fdot(feat_b, theta_b))).astype(jnp.bfloat16))
        weighted2 = rounded.astype(jnp.float32)
        lead = theta_b[1:1 + count]
        blocks = (theta_b[pair_table.reshape(-1)].astype(jnp.float32) * doubling.reshape(-1, 1)).astype(jnp.bfloat16)
        blocks = blocks.reshape(count, count, theta.shape[1])

        def per_label(item):
            linear, block = item
            jac = linear.astype(jnp.float32)[None, :] + fdot(lab_b, block)
            return jnp.sum(weighted2 * jac, axis=1), jnp.sum(ivar_f * jac * jac, axis=1)

        grads, curvs = lax.map(per_label, (lead, blocks))
        lgrad = grads.T - lab
        lcurv = 1.0 + curvs.T
        lab = lab + lgrad / lcurv
    return theta, lab
```

```python
import functools

import jax
import jax.numpy as jnp
import numpy as np
from jax import lax
from jax.experimental import pallas as pl
from jax.experimental.pallas import tpu as pltpu
from jax.sharding import PartitionSpec as P

ALTS = 2
STEP = 0.25
NX, NZ, NY = 4, 16, 4
F = 256
BP = 256
CH = 16
KL = 32
MESH = pl.DeviceIdType.MESH
BF = jnp.bfloat16
F32 = jnp.float32


def tables(count):
    left = np.full((F,), -1, np.int32)
    right = np.full((F,), -1, np.int32)
    left[0] = right[0] = count
    for m in range(count):
        left[1 + m], right[1 + m] = m, count
    pos = 1 + count
    pair = np.zeros((count, count), np.int32)
    for i in range(count):
        for j in range(i, count):
            left[pos], right[pos] = i, j
            pair[i, j] = pair[j, i] = pos
            pos += 1
    sl = np.zeros((128, F), np.float32)
    sr = np.zeros((128, F), np.float32)
    for f in range(pos):
        sl[left[f], f] = 1.0
        sr[right[f], f] = 1.0
    pick = np.zeros((count * KL, F), np.float32)
    for m in range(count):
        for j in range(count):
            pick[m * KL + j, pair[m, j]] = 2.0 if j == m else 1.0
        pick[m * KL + count, 1 + m] = 1.0
    back_l = sl.T.copy()
    back_r = sr.T.copy()
    back_l[:, count:] = 0.0
    back_r[:, count:] = 0.0
    cols = np.concatenate([sl, sr], axis=1)
    rows_l = np.concatenate([sl.T, sl.T], axis=0)
    rows_r = np.concatenate([sr.T, sr.T], axis=0)
    return [jnp.asarray(t, BF) for t in (cols, rows_l, rows_r, pick, back_l, back_r)]


def nn(a, b):
    return lax.dot_general(a, b, (((1,), (0,)), ((), ())), preferred_element_type=F32)


def nt(a, b):
    return lax.dot_general(a, b, (((1,), (1,)), ((), ())), preferred_element_type=F32)


def three(v):
    hi = v.astype(BF)
    rest = v - hi.astype(F32)
    mid = rest.astype(BF)
    low = (rest - mid.astype(F32)).astype(BF)
    return hi, mid, low


def kernel(
    count, stars, flux, ivar, coeffs, labt, cols, rows_l, rows_r, pick, back_l, back_r,
    theta_out, lab_out,
    th, thb, lt, fb, ftb, sqt, selh, labb, iv, ivf, w, part, xs, g_acc, tall, ac, lgc,
    xr1a, xr1b, xr2l, xr2r, zfp, zfm, zrl, zr, halves, p1, yb, fin,
    sxs, sxr, szs, szr, sas, sar, sbs, sbr, sps, spr,
):
    star = lax.axis_index("star")
    pix = lax.axis_index("pix")
    x, z = star // NZ, star % NZ
    y, core = pix // 2, pix % 2

    def star_at(dx, dz):
        return {"star": ((x + dx) % NX) * NZ + (z + dz) % NZ}

    right, left = star_at(1, 0), star_at(NX - 1, 0)
    partner = {"pix": y * 2 + 1 - core}

    def along_z(d):
        return star_at(0, d % NZ)

    def along_y(d):
        return {"pix": ((y + d) % NY) * 2 + core}

    def rcopy(src, dst, ssem, rsem, dev):
        return pltpu.make_async_remote_copy(
            src_ref=src, dst_ref=dst, send_sem=ssem, recv_sem=rsem,
            device_id=dev, device_id_type=MESH,
        )

    zpeers = (1, 2, 3, 4, -1, -2, -3, -4)
    peers = [right, left, partner] + [along_z(d) for d in zpeers] + [along_y(d) for d in (1, 2, 3)]
    barrier = pltpu.get_barrier_semaphore()
    for peer in peers:
        pl.semaphore_signal(barrier, inc=1, device_id=peer, device_id_type=MESH)

    def px(blk):
        return pl.ds(pl.multiple_of(blk * BP, BP), BP)

    def px_half(blk, half):
        return pl.ds(pl.multiple_of(blk * BP + half * 128, 128), 128)

    nfeat = coeffs.shape[0]
    th[0, pl.ds(F - 32, 32), :] = jnp.zeros((32, th.shape[2]), F32)
    th[0, pl.ds(0, nfeat), :] = coeffs[...]
    thb[...] = th[0].astype(BF)
    lt[...] = labt[...]
    iv[pl.ds(0, stars), :] = ivar[...]
    iv[pl.ds(stars, iv.shape[0] - stars), :] = jnp.zeros((iv.shape[0] - stars, iv.shape[1]), BF)
    ivf[...] = ivar[...].astype(F32)
    w[pl.ds(stars, w.shape[0] - stars), :] = jnp.zeros((w.shape[0] - stars, w.shape[1]), BF)
    lgc[...] = jnp.zeros(lgc.shape, F32)

    blk_o, blk_r, blk_l = (x + 2) % NX, (x + 1) % NX, (x + 3) % NX
    zrot = pl.multiple_of(((z + NZ - 3) % NZ) * CH, CH)

    def weigh(blk):
        model = nn(fb[...], thb[:, px(blk)])
        return (ivf[:, px(blk)] * (flux[:, px(blk)].astype(F32) - model)).astype(BF)

    def turn_body(turn, carry):
        ltv = lt[...]
        hi, mid, low = three(ltv)
        ahi, amid, alow = three(ltv.T)
        sel = nn(ahi, cols[...])
        selh[...] = sel[:stars].astype(BF)
        labb[...] = ahi[:stars, :KL]
        full = sel + nn(amid, cols[...]) + nn(alow, cols[...])
        fb[...] = (full[:stars, :F] * full[:stars, F:]).astype(BF)
        rl, rr = rows_l[pl.ds(zrot, F), :], rows_r[pl.ds(zrot, F), :]
        featt = (nn(rl, hi) + nn(rl, mid) + nn(rl, low)) * (nn(rr, hi) + nn(rr, mid) + nn(rr, low))
        ftb[...] = featt.astype(BF)
        sqt[...] = (featt * featt).astype(BF)

        def grads(blk):
            w[pl.ds(0, stars), px(blk)] = weigh(blk)
            part[turn, 0, :, px(blk)] = nn(ftb[...], w[:, px(blk)])
            part[turn, 1, :, px(blk)] = nn(sqt[...], iv[:, px(blk)])

        rows = lambda k: pl.ds(64 * k, 64)
        groups = (2, 3, 1, 0)

        def xcopy(n, k):
            src = part.at[turn]
            s, r = sxs.at[turn, n, k], sxr.at[turn, n, k]
            if n == 0:
                return rcopy(src.at[:, rows(k), px_half(blk_o, 0)], xr1a.at[turn, k], s, r, right)
            if n == 1:
                return rcopy(src.at[:, rows(k), px_half(blk_o, 1)], xr1b.at[turn, k], s, r, left)
            if n == 2:
                return rcopy(src.at[:, rows(k), px_half(blk_r, 1)], xr2l.at[turn, k, 1], s, r, right)
            if n == 3:
                return rcopy(src.at[:, rows(k), px_half(blk_l, 0)], xr2r.at[turn, k, 0], s, r, left)
            if n == 4:
                return rcopy(src.at[:, rows(k), px_half(blk_r, 0)], xr2l.at[turn, k, 0], s, r, right)
            return rcopy(src.at[:, rows(k), px_half(blk_l, 1)], xr2r.at[turn, k, 1], s, r, left)

        grads(blk_o)

        @pl.when(turn == 0)
        def _():
            pl.semaphore_wait(barrier, len(peers))

        for k in groups:
            xcopy(0, k).start()
            xcopy(1, k).start()
        grads(blk_r)
        for k in groups:
            xcopy(2, k).start()
        grads(blk_l)
        for k in groups:
            xcopy(3, k).start()
        grads(x)

        def relay_x(k):
            xcopy(0, k).wait_recv()
            a = px_half(blk_r, 0)
            part[turn, :, rows(k), a] = part[turn, :, rows(k), a] + xr1a[turn, k]
            xcopy(4, k).start()
            xcopy(1, k).wait_recv()
            b = px_half(blk_l, 1)
            part[turn, :, rows(k), b] = part[turn, :, rows(k), b] + xr1b[turn, k]
            xcopy(5, k).start()

        def finish_x(k):
            for n in (2, 3, 4, 5):
                xcopy(n, k).wait_recv()
            for h in (0, 1):
                xs[turn, :, rows(k), pl.ds(128 * h, 128)] = (
                    part[turn, :, rows(k), px_half(x, h)] + xr2l[turn, k, h] + xr2r[turn, k, h]
                )

        def chunk(d):
            return xs.at[turn, :, pl.ds(CH * ((d + 3) % NZ), CH), :]

        zd = {1: 0, 2: 1, 3: 2, -1: 3, -2: 4, -3: 5, 4: 6, -4: 7, 5: 8, 6: 9, 7: 10, 8: 11, -5: 12, -6: 13, -7: 14}

        def zcopy(d):
            s, r = szs.at[turn, zd[d]], szr.at[turn, zd[d]]
            if d > 4:
                return rcopy(chunk(d), zfp.at[turn, d - 5], s, r, along_z(d - 4))
            if d < -4:
                return rcopy(chunk(d), zfm.at[turn, -d - 5], s, r, along_z(d + 4))
            src = chunk(d) if abs(d) < 4 else zrl.at[turn, 0 if d > 0 else 1]
            return rcopy(src, zr.at[turn, zd[d]], s, r, along_z(d))

        relay_x(2)
        relay_x(3)
        finish_x(2)
        for d in (8, 7, 6, 5):
            zcopy(d).start()
        relay_x(1)
        finish_x(3)
        for d in (-7, -6, -5):
            zcopy(d).start()
        relay_x(0)
        finish_x(1)
        for d in (8, 7, 6, 5):
            zcopy(d).wait_recv()
        zrl[turn, 0] = chunk(4)[...] + ((zfp[turn, 0] + zfp[turn, 1]) + (zfp[turn, 2] + zfp[turn, 3]))
        zcopy(4).start()
        for d in (3, 2, 1):
            zcopy(d).start()
        for d in (-7, -6, -5):
            zcopy(d).wait_recv()
        zrl[turn, 1] = chunk(-4)[...] + ((zfm[turn, 0] + zfm[turn, 1]) + zfm[turn, 2])
        zcopy(-4).start()
        finish_x(0)
        for d in (-3, -2, -1):
            zcopy(d).start()
        for d in (3, 2, 1, -3, -2, -1, 4, -4):
            zcopy(d).wait_recv()
        total = chunk(0)[...]
        for i in range(8):
            total = total + zr[turn, i]
        mine = pl.ds(pl.multiple_of(z * CH, CH), CH)
        th[turn + 1, mine, px(x)] = th[turn, mine, px(x)] + STEP * total[0] / (1.0 + total[1])

        def srows(d):
            return pl.ds(pl.multiple_of(((z - d) % NZ) * CH, CH), CH)

        new = th.at[turn + 1]

        def acopy(d):
            s, r = sas.at[turn, zd[d]], sar.at[turn, zd[d]]
            if abs(d) <= 4:
                ref = new.at[mine, px(x)]
                return rcopy(ref, ref, s, r, along_z(d))
            hop = d - 4 if d > 0 else d + 4
            ref = new.at[srows(4 if d > 0 else -4), px(x)]
            return rcopy(ref, ref, s, r, along_z(hop))

        def bcopy(n, d):
            s, r = sbs.at[turn, n, d % NZ], sbr.at[turn, n, d % NZ]
            if n < 2:
                ref = new.at[srows(d), px(x)]
            elif n == 2:
                ref = new.at[srows(d), px_half(blk_l, 0)]
            else:
                ref = new.at[srows(d), px_half(blk_r, 1)]
            return rcopy(ref, ref, s, r, right if n % 2 == 0 else left)

        for d in (4, -4, 3, -3, 2, -2, 1, -1):
            acopy(d).start()
        bcopy(0, 0).start()
        bcopy(1, 0).start()
        arrivals = (1, -1, 2, -2, 3, -3, 4, -4, 5, -5, 6, -6, 7, -7, 8)
        for d in arrivals:
            acopy(d).wait_recv()
            if d == 4:
                for e in (8, 7, 6, 5):
                    acopy(e).start()
            if d == -4:
                for e in (-7, -6, -5):
                    acopy(e).start()
            bcopy(0, d).start()
            bcopy(1, d).start()

        g_acc[...] = jnp.zeros(g_acc.shape, F32)
        ac[...] = jnp.zeros(ac.shape, F32)

        def label_block(blk):
            thb[:, px(blk)] = th[turn + 1, :, px(blk)].astype(BF)
            t = thb[:, px(blk)]
            g_acc[...] = g_acc[...] + nt(weigh(blk), t)
            tall[...] = nn(pick[...], t).astype(BF)

            def one(m, c):
                jac = nn(labb[...], tall[pl.ds(pl.multiple_of(m * KL, KL), KL), :])
                q = ivf[:, px(blk)] * jac * jac
                ac[m] = ac[m] + q[:, :128] + q[:, 128:]
                return c

            lax.fori_loop(0, count, one, 0)

        every = (0,) + arrivals
        for d in every:
            bcopy(0, d).wait_recv()
            bcopy(2, d).start()
            bcopy(1, d).wait_recv()
            bcopy(3, d).start()
        label_block(x)
        label_block(blk_l)
        label_block(blk_r)
        for d in every:
            bcopy(2, d).wait_recv()
            bcopy(3, d).wait_recv()
        label_block(blk_o)

        sel_l, sel_r = selh[:, :F].astype(F32), selh[:, F:].astype(F32)
        lg = jnp.zeros((stars, 128), F32)
        for h, back in ((g_acc[...] * sel_r, back_l), (g_acc[...] * sel_l, back_r)):
            h0 = h.astype(BF)
            h1 = (h - h0.astype(F32)).astype(BF)
            lg = lg + nn(h0, back[...]) + nn(h1, back[...])
        lgc[pl.ds(0, stars), :] = lg
        lane = lax.broadcasted_iota(jnp.int32, (stars, 128), 1)

        def put(m, c):
            tot = jnp.sum(ac[m], axis=1, keepdims=True)
            lgc[pl.ds(0, stars), :] = jnp.where(lane == 24 + m, tot, lgc[pl.ds(0, stars), :])
            return c

        lax.fori_loop(0, count, put, 0)
        sums = lgc[...].T
        halves[turn, 0] = sums[0:24]
        halves[turn, 1] = sums[24:48]

        def pcopy(n):
            s, r = sps.at[turn, n], spr.at[turn, n]
            if n == 0:
                return rcopy(halves.at[turn, 1 - core], p1.at[turn], s, r, partner)
            if n == 4:
                ref = fin.at[turn, core]
                return rcopy(ref, ref, s, r, partner)
            ref = yb.at[turn, y]
            return rcopy(ref, ref, s, r, along_y(n))

        pcopy(0).start()
        pcopy(0).wait_recv()
        yb[turn, y] = halves[turn, core] + p1[turn]
        for n in (2, 1, 3):
            pcopy(n).start()
        for n in (1, 2, 3):
            pcopy(n).wait_recv()
        fin[turn, core] = (yb[turn, 0] + yb[turn, 1]) + (yb[turn, 2] + yb[turn, 3])
        pcopy(4).start()
        pcopy(4).wait_recv()
        lab = lt[pl.ds(0, 24), :]
        row = lax.broadcasted_iota(jnp.int32, lab.shape, 0)
        lt[pl.ds(0, 24), :] = jnp.where(row < count, lab + (fin[turn, 0] - lab) / (1.0 + fin[turn, 1]), lab)

        for k in groups:
            for n in range(6):
                xcopy(n, k).wait_send()
        for d in zd:
            zcopy(d).wait_send()
            acopy(d).wait_send()
        for d in every:
            for n in range(4):
                bcopy(n, d).wait_send()
        for n in range(5):
            pcopy(n).wait_send()
        return carry

    lax.fori_loop(0, ALTS, turn_body, 0)
    theta_out[...] = th[ALTS, pl.ds(0, nfeat), :]
    lab_out[...] = lt[...].T[:stars, :count]


def per_device(flux, inv_var, coeffs, labels):
    stars, count = labels.shape
    pixels = flux.shape[1]
    nfeat = coeffs.shape[0]
    wide = -(-stars // 128) * 128
    labt = jnp.zeros((128, wide), F32)
    labt = labt.at[:count, :stars].set(labels.T).at[count, :stars].set(1.0)
    dma = pltpu.SemaphoreType.DMA
    scratch = [
        pltpu.VMEM((ALTS + 1, F, pixels), F32),
        pltpu.VMEM((F, pixels), BF),
        pltpu.VMEM((128, wide), F32),
        pltpu.VMEM((stars, F), BF),
        pltpu.VMEM((F, wide), BF),
        pltpu.VMEM((F, wide), BF),
        pltpu.VMEM((stars, 2 * F), BF),
        pltpu.VMEM((stars, KL), BF),
        pltpu.VMEM((wide, pixels), BF),
        pltpu.VMEM((stars, pixels), F32),
        pltpu.VMEM((wide, pixels), BF),
        pltpu.VMEM((ALTS, 2, F, pixels), F32),
        pltpu.VMEM((ALTS, 2, F, BP), F32),
        pltpu.VMEM((stars, F), F32),
        pltpu.VMEM((count * KL, BP), BF),
        pltpu.VMEM((count, stars, 128), F32),
        pltpu.VMEM((wide, 128), F32),
        pltpu.VMEM((ALTS, 4, 2, 64, 128), F32),
        pltpu.VMEM((ALTS, 4, 2, 64, 128), F32),
        pltpu.VMEM((ALTS, 4, 2, 2, 64, 128), F32),
        pltpu.VMEM((ALTS, 4, 2, 2, 64, 128), F32),
        pltpu.VMEM((ALTS, 4, 2, CH, BP), F32),
        pltpu.VMEM((ALTS, 3, 2, CH, BP), F32),
        pltpu.VMEM((ALTS, 2, 2, CH, BP), F32),
        pltpu.VMEM((ALTS, 8, 2, CH, BP), F32),
        pltpu.VMEM((ALTS, 2, 24, wide), F32),
        pltpu.VMEM((ALTS, 24, wide), F32),
        pltpu.VMEM((ALTS, NY, 24, wide), F32),
        pltpu.VMEM((ALTS, 2, 24, wide), F32),
        dma((ALTS, 6, 4)), dma((ALTS, 6, 4)),
        dma((ALTS, 15)), dma((ALTS, 15)),
        dma((ALTS, 15)), dma((ALTS, 15)),
        dma((ALTS, 4, NZ)), dma((ALTS, 4, NZ)),
        dma((ALTS, 5)), dma((ALTS, 5)),
    ]
    vmem = pl.BlockSpec(memory_space=pltpu.VMEM)
    return pl.pallas_call(
        functools.partial(kernel, count, stars),
        out_shape=(
            jax.ShapeDtypeStruct((nfeat, pixels), F32),
            jax.ShapeDtypeStruct((stars, count), F32),
        ),
        in_specs=[vmem] * 10,
        out_specs=(vmem, vmem),
        scratch_shapes=scratch,
        compiler_params=pltpu.CompilerParams(
            collective_id=0, has_side_effects=True, vmem_limit_bytes=60 * 1024 * 1024
        ),
    )(flux, inv_var, coeffs, labt, *tables(count))


def solution(mesh):
    return jax.shard_map(
        per_device,
        mesh=mesh,
        in_specs=(P("star", "pix"), P("star", "pix"), P(None, "pix"), P("star", None)),
        out_specs=(P(None, "pix"), P("star", None)),
        check_vma=False,
    )
```

```python
import functools

import jax
import jax.numpy as jnp
import numpy as np
from jax import lax
from jax.experimental import pallas as pl
from jax.experimental.pallas import tpu as pltpu
from jax.sharding import PartitionSpec as P

ALTS = 2
STEP = 0.25
NX, NZ, NY = 4, 16, 4
F = 256
BP = 256
CH = 16
KL = 32
MESH = pl.DeviceIdType.MESH
BF = jnp.bfloat16
F32 = jnp.float32


def tables(count):
    left = np.full((F,), -1, np.int32)
    right = np.full((F,), -1, np.int32)
    left[0] = right[0] = count
    for m in range(count):
        left[1 + m], right[1 + m] = m, count
    pos = 1 + count
    pair = np.zeros((count, count), np.int32)
    for i in range(count):
        for j in range(i, count):
            left[pos], right[pos] = i, j
            pair[i, j] = pair[j, i] = pos
            pos += 1
    sl = np.zeros((128, F), np.float32)
    sr = np.zeros((128, F), np.float32)
    for f in range(pos):
        sl[left[f], f] = 1.0
        sr[right[f], f] = 1.0
    pick = np.zeros((count * KL, F), np.float32)
    for m in range(count):
        for j in range(count):
            pick[m * KL + j, pair[m, j]] = 2.0 if j == m else 1.0
        pick[m * KL + count, 1 + m] = 1.0
    back_l = sl.T.copy()
    back_r = sr.T.copy()
    back_l[:, count:] = 0.0
    back_r[:, count:] = 0.0
    cols = np.zeros((128, 2 * F), np.float32)
    for t in range(3):
        cols[24 * t : 24 * t + 24] = np.concatenate([sl, sr], axis=1)[:24]
    rows_l, rows_r = cols[:, :F].T, cols[:, F:].T
    twice = lambda t: np.concatenate([t, t], axis=0)
    mats = (cols, twice(rows_l), twice(rows_r), pick, twice(back_l), twice(back_r))
    return [jnp.asarray(t, BF) for t in mats]


def nn(a, b):
    return lax.dot_general(a, b, (((1,), (0,)), ((), ())), preferred_element_type=F32)


def nt(a, b):
    return lax.dot_general(a, b, (((1,), (1,)), ((), ())), preferred_element_type=F32)


def three(v):
    hi = v.astype(BF)
    rest = v - hi.astype(F32)
    mid = rest.astype(BF)
    low = (rest - mid.astype(F32)).astype(BF)
    return hi, mid, low


def kernel(
    count, stars, flux, ivar, coeffs, labels, cols, rows_l, rows_r, pick, back_l, back_r,
    theta_out, lab_out,
    th, thb, lt, colsr, pickr, fb, ftb, sqt, selh, labb, iv, ivf, w, part, xs, g_acc, tall, ac, lgc,
    xr1a, xr1b, xr2l, xr2r, zfp, zfm, zrl, zr, halves, p1, yb, fin,
    sxs, sxr, szs, szr, sas, sar, sbs, sbr, sps, spr,
):
    star = lax.axis_index("star")
    pix = lax.axis_index("pix")
    x, z = star // NZ, star % NZ
    y, core = pix // 2, pix % 2

    def star_at(dx, dz):
        return {"star": ((x + dx) % NX) * NZ + (z + dz) % NZ}

    right, left = star_at(1, 0), star_at(NX - 1, 0)
    partner = {"pix": y * 2 + 1 - core}

    def along_z(d):
        return star_at(0, d % NZ)

    def along_y(d):
        return {"pix": ((y + d) % NY) * 2 + core}

    def rcopy(src, dst, ssem, rsem, dev):
        return pltpu.make_async_remote_copy(
            src_ref=src, dst_ref=dst, send_sem=ssem, recv_sem=rsem,
            device_id=dev, device_id_type=MESH,
        )

    zpeers = (1, 2, 3, 4, -1, -2, -3, -4)
    peers = [right, left, partner] + [along_z(d) for d in zpeers] + [along_y(d) for d in (1, 2, 3)]
    barrier = pltpu.get_barrier_semaphore()
    for peer in peers:
        pl.semaphore_signal(barrier, inc=1, device_id=peer, device_id_type=MESH)

    def px(blk):
        return pl.ds(pl.multiple_of(blk * BP, BP), BP)

    def px_half(blk, half):
        return pl.ds(pl.multiple_of(blk * BP + half * 128, 128), 128)

    def pos(d):
        return CH * ((d + 3) % NZ)

    def at_row(chunk):
        return pl.ds(pl.multiple_of(((chunk - z + 3 + NZ) % NZ) * CH, CH), CH)

    first = (z + NZ - 3) % NZ
    zrot = pl.multiple_of(first * CH, CH)
    nfeat, pixels = coeffs.shape
    for c in range(NZ):
        have = min(max(nfeat - c * CH, 0), CH)
        rows = coeffs[pl.ds(c * CH, have), :] if have else jnp.zeros((CH, pixels), F32)
        if 0 < have < CH:
            rows = jnp.concatenate([rows, jnp.zeros((CH - have, pixels), F32)], axis=0)
        th[0, at_row(c), :] = rows
        thb[at_row(c), :] = rows.astype(BF)
    wide = lt.shape[1]
    lt[...] = jnp.zeros(lt.shape, F32)
    lt[pl.ds(0, count), pl.ds(0, stars)] = labels[...]
    lt[pl.ds(count, 1), pl.ds(0, stars)] = jnp.ones((1, stars), F32)
    iv[pl.ds(0, stars), :] = ivar[...]
    iv[pl.ds(stars, wide - stars), :] = jnp.zeros((wide - stars, pixels), BF)
    ivf[...] = ivar[...].astype(F32)
    w[pl.ds(stars, wide - stars), :] = jnp.zeros((wide - stars, pixels), BF)
    lgc[...] = jnp.zeros(lgc.shape, F32)
    back = (F - zrot) % F
    for h in (0, F):
        colsr[:, pl.ds(h, F)] = pltpu.roll(cols[:, pl.ds(h, F)].astype(F32), back, 1).astype(BF)
    pickr[...] = pltpu.roll(pick[...].astype(F32), back, 1).astype(BF)

    blk_o, blk_r, blk_l = (x + 2) % NX, (x + 1) % NX, (x + 3) % NX
    lane = lax.broadcasted_iota(jnp.int32, (stars, 128), 1)
    zd = {1: 0, 2: 1, 3: 2, -1: 3, -2: 4, -3: 5, 4: 6, -4: 7, 5: 8, 6: 9, 7: 10, 8: 11, -5: 12, -6: 13, -7: 14}
    groups = (2, 3, 1, 0)

    def rows(k):
        return pl.ds(64 * k, 64)

    def weigh(blk):
        model = nn(fb[...], thb[:, px(blk)])
        return (ivf[:, px(blk)] * (flux[:, px(blk)].astype(F32) - model)).astype(BF)

    def turn_body(turn, carry):
        hi, mid, low = three(lt[...])
        stack = jnp.concatenate(
            [hi.astype(F32), mid.astype(F32), low.astype(F32), jnp.zeros((128 - 72, wide), F32)], axis=0
        )
        stack_b = stack.astype(BF)
        stack_t = stack.T.astype(BF)
        featt = nn(rows_l[pl.ds(zrot, F), :], stack_b) * nn(rows_r[pl.ds(zrot, F), :], stack_b)
        ftb[...] = featt.astype(BF)
        sqt[...] = (featt * featt).astype(BF)
        full = nn(stack_t[:stars], colsr[...])
        fb[...] = (full[:, :F] * full[:, F:]).astype(BF)
        selh[...] = full.astype(BF)
        labb[...] = stack_t[:stars, :KL]

        def grads(blk):
            part[turn, 1, :, px(blk)] = nn(sqt[...], iv[:, px(blk)])
            w[pl.ds(0, stars), px(blk)] = weigh(blk)
            part[turn, 0, :, px(blk)] = nn(ftb[...], w[:, px(blk)])

        def xcopy(n, k):
            src = part.at[turn]
            s, r = sxs.at[turn, n, k], sxr.at[turn, n, k]
            if n == 0:
                return rcopy(src.at[:, rows(k), px_half(blk_o, 0)], xr1a.at[turn, k], s, r, right)
            if n == 1:
                return rcopy(src.at[:, rows(k), px_half(blk_o, 1)], xr1b.at[turn, k], s, r, left)
            if n == 2:
                return rcopy(src.at[:, rows(k), px_half(blk_r, 1)], xr2l.at[turn, k, 1], s, r, right)
            if n == 3:
                return rcopy(src.at[:, rows(k), px_half(blk_l, 0)], xr2r.at[turn, k, 0], s, r, left)
            if n == 4:
                return rcopy(src.at[:, rows(k), px_half(blk_r, 0)], xr2l.at[turn, k, 0], s, r, right)
            return rcopy(src.at[:, rows(k), px_half(blk_l, 1)], xr2r.at[turn, k, 1], s, r, left)

        def send_x(k, pair):
            xcopy(pair, k).start()
            xcopy(pair + 1, k).start()

        def relay_x(k):
            xcopy(0, k).wait_recv()
            a = px_half(blk_r, 0)
            part[turn, :, rows(k), a] = part[turn, :, rows(k), a] + xr1a[turn, k]
            xcopy(4, k).start()
            xcopy(1, k).wait_recv()
            b = px_half(blk_l, 1)
            part[turn, :, rows(k), b] = part[turn, :, rows(k), b] + xr1b[turn, k]
            xcopy(5, k).start()

        def finish_x(k):
            for n in (2, 3, 4, 5):
                xcopy(n, k).wait_recv()
            for h in (0, 1):
                xs[turn, :, rows(k), pl.ds(128 * h, 128)] = (
                    part[turn, :, rows(k), px_half(x, h)] + xr2l[turn, k, h] + xr2r[turn, k, h]
                )

        def chunk(d):
            return xs.at[turn, :, pl.ds(pos(d), CH), :]

        def zcopy(d):
            s, r = szs.at[turn, zd[d]], szr.at[turn, zd[d]]
            if d > 4:
                return rcopy(chunk(d), zfp.at[turn, d - 5], s, r, along_z(d - 4))
            if d < -4:
                return rcopy(chunk(d), zfm.at[turn, -d - 5], s, r, along_z(d + 4))
            src = chunk(d) if abs(d) < 4 else zrl.at[turn, 0 if d > 0 else 1]
            return rcopy(src, zr.at[turn, zd[d]], s, r, along_z(d))

        grads(blk_o)

        @pl.when(turn == 0)
        def _():
            pl.semaphore_wait(barrier, len(peers))

        g0, g1, g2, g3 = groups
        send_x(g0, 0)
        send_x(g1, 0)
        grads(blk_r)
        grads(blk_l)
        send_x(g0, 2)
        send_x(g1, 2)
        relay_x(g0)
        send_x(g2, 0)
        send_x(g2, 2)
        grads(x)
        relay_x(g1)
        send_x(g3, 0)
        send_x(g3, 2)
        finish_x(g0)
        for d in (8, 7, 6, 5):
            zcopy(d).start()
        relay_x(g2)
        finish_x(g1)
        for d in (-7, -6, -5):
            zcopy(d).start()
        relay_x(g3)
        finish_x(g2)
        for d in (8, 7, 6, 5):
            zcopy(d).wait_recv()
        zrl[turn, 0] = chunk(4)[...] + ((zfp[turn, 0] + zfp[turn, 1]) + (zfp[turn, 2] + zfp[turn, 3]))
        zcopy(4).start()
        for d in (3, 2, 1):
            zcopy(d).start()
        for d in (-7, -6, -5):
            zcopy(d).wait_recv()
        zrl[turn, 1] = chunk(-4)[...] + ((zfm[turn, 0] + zfm[turn, 1]) + zfm[turn, 2])
        zcopy(-4).start()
        finish_x(g3)
        for d in (-3, -2, -1):
            zcopy(d).start()
        for d in (3, 2, 1, -3, -2, -1, 4, -4):
            zcopy(d).wait_recv()
        total = chunk(0)[...]
        for i in range(8):
            total = total + zr[turn, i]
        mine = pl.ds(pos(0), CH)
        th[turn + 1, mine, px(x)] = th[turn, mine, px(x)] + STEP * total[0] / (1.0 + total[1])

        new = th.at[turn + 1]

        def acopy(d):
            s, r = sas.at[turn, zd[d]], sar.at[turn, zd[d]]
            if abs(d) <= 4:
                src, dst, hop = pos(0), pos(-d), d
            else:
                hop = d - 4 if d > 0 else d + 4
                src, dst = pos(-4 if d > 0 else 4), pos(-d)
            return rcopy(
                new.at[pl.ds(src, CH), px(x)], new.at[pl.ds(dst, CH), px(x)], s, r, along_z(hop)
            )

        def bcopy(n, k):
            s, r = sbs.at[turn, n, k], sbr.at[turn, n, k]
            if n < 2:
                ref = new.at[rows(k), px(x)]
            elif n == 2:
                ref = new.at[rows(k), px_half(blk_l, 0)]
            else:
                ref = new.at[rows(k), px_half(blk_r, 1)]
            return rcopy(ref, ref, s, r, right if n % 2 == 0 else left)

        def spread(k):
            bcopy(0, k).start()
            bcopy(1, k).start()

        def pass_on(k):
            bcopy(0, k).wait_recv()
            bcopy(2, k).start()
            bcopy(1, k).wait_recv()
            bcopy(3, k).start()

        for d in (4, -4, 3, -3, 2, -2, 1, -1):
            acopy(d).start()
        acopy(4).wait_recv()
        for e in (8, 7, 6, 5):
            acopy(e).start()
        acopy(-4).wait_recv()
        for e in (-7, -6, -5):
            acopy(e).start()
        for d in (3, 2, 1):
            acopy(d).wait_recv()
        spread(0)
        for d in (-3, -2, -1):
            acopy(d).wait_recv()
        spread(1)
        pass_on(0)
        pass_on(1)
        for d in (5, 6, 7):
            acopy(d).wait_recv()
        spread(3)
        for d in (-5, -6, -7, 8):
            acopy(d).wait_recv()
        spread(2)

        def label_block(blk, place, between=None):
            thb[:, px(blk)] = th[turn + 1, :, px(blk)].astype(BF)
            t = thb[:, px(blk)]
            part_g = nt(weigh(blk), t)
            g_acc[...] = part_g if place == 0 else g_acc[...] + part_g
            tall[...] = nn(pickr[...], t).astype(BF)

            def some(i, c):
                for u in range(4):
                    m = 4 * i + u
                    jac = nn(labb[...], tall[pl.ds(pl.multiple_of(m * KL, KL), KL), :])
                    q = ivf[:, px(blk)] * jac * jac
                    q = q[:, :128] + q[:, 128:]
                    if place > 0:
                        q = ac[m] + q
                    if place < 3:
                        ac[m] = q
                    else:
                        tot = jnp.sum(q, axis=1, keepdims=True)
                        lgc[pl.ds(0, stars), :] = jnp.where(lane == 24 + m, tot, lgc[pl.ds(0, stars), :])
                return c

            if between is None:
                lax.fori_loop(0, count // 4, some, 0)
            else:
                lax.fori_loop(0, 2, some, 0)
                between()
                lax.fori_loop(2, count // 4, some, 0)

        label_block(x, 0, lambda: pass_on(3))
        pass_on(2)
        label_block(blk_l, 1)
        label_block(blk_r, 2)
        for k in range(4):
            bcopy(2, k).wait_recv()
            bcopy(3, k).wait_recv()
        label_block(blk_o, 3)

        lg = jnp.zeros((stars, 128), F32)
        for h, table in ((selh[:, F:], back_l), (selh[:, :F], back_r)):
            h = g_acc[...] * h.astype(F32)
            h0 = h.astype(BF)
            h1 = (h - h0.astype(F32)).astype(BF)
            b = table[pl.ds(zrot, F), :]
            lg = lg + nn(h0, b) + nn(h1, b)
        low_lanes = lane < 24
        lgc[pl.ds(0, stars), :] = jnp.where(low_lanes, lg, lgc[pl.ds(0, stars), :])
        sums = lgc[...].T
        halves[turn, 0] = sums[0:24]
        halves[turn, 1] = sums[24:48]

        def pcopy(n):
            s, r = sps.at[turn, n], spr.at[turn, n]
            if n == 0:
                return rcopy(halves.at[turn, 1 - core], p1.at[turn], s, r, partner)
            if n == 4:
                ref = fin.at[turn, core]
                return rcopy(ref, ref, s, r, partner)
            ref = yb.at[turn, y]
            return rcopy(ref, ref, s, r, along_y(n))

        pcopy(0).start()
        pcopy(0).wait_recv()
        yb[turn, y] = halves[turn, core] + p1[turn]
        for n in (2, 1, 3):
            pcopy(n).start()

        @pl.when(turn == ALTS - 1)
        def _():
            for c in range(NZ):
                have = min(max(nfeat - c * CH, 0), CH)
                if have:
                    theta_out[pl.ds(c * CH, have), :] = new[at_row(c), :][:have]

        for n in (1, 2, 3):
            pcopy(n).wait_recv()
        fin[turn, core] = (yb[turn, 0] + yb[turn, 1]) + (yb[turn, 2] + yb[turn, 3])
        pcopy(4).start()
        pcopy(4).wait_recv()
        lab = lt[...]
        row = lax.broadcasted_iota(jnp.int32, lab.shape, 0)
        lt[...] = jnp.where(row < count, lab + (fin[turn, 0] - lab) / (1.0 + fin[turn, 1]), lab)

        for k in groups:
            for n in range(6):
                xcopy(n, k).wait_send()
            for n in range(4):
                bcopy(n, k).wait_send()
        for d in zd:
            zcopy(d).wait_send()
            acopy(d).wait_send()
        for n in range(5):
            pcopy(n).wait_send()
        return carry

    lax.fori_loop(0, ALTS, turn_body, 0)
    lab_out[...] = lt[pl.ds(0, count), pl.ds(0, stars)]


def per_device(flux, inv_var, coeffs, labels):
    stars, count = labels.shape
    pixels = flux.shape[1]
    nfeat = coeffs.shape[0]
    wide = -(-stars // 128) * 128
    dma = pltpu.SemaphoreType.DMA
    scratch = [
        pltpu.VMEM((ALTS + 1, F, pixels), F32),
        pltpu.VMEM((F, pixels), BF),
        pltpu.VMEM((24, wide), F32),
        pltpu.VMEM((128, 2 * F), BF),
        pltpu.VMEM((count * KL, F), BF),
        pltpu.VMEM((stars, F), BF),
        pltpu.VMEM((F, wide), BF),
        pltpu.VMEM((F, wide), BF),
        pltpu.VMEM((stars, 2 * F), BF),
        pltpu.VMEM((stars, KL), BF),
        pltpu.VMEM((wide, pixels), BF),
        pltpu.VMEM((stars, pixels), F32),
        pltpu.VMEM((wide, pixels), BF),
        pltpu.VMEM((ALTS, 2, F, pixels), F32),
        pltpu.VMEM((ALTS, 2, F, BP), F32),
        pltpu.VMEM((stars, F), F32),
        pltpu.VMEM((count * KL, BP), BF),
        pltpu.VMEM((count, stars, 128), F32),
        pltpu.VMEM((wide, 128), F32),
        pltpu.VMEM((ALTS, 4, 2, 64, 128), F32),
        pltpu.VMEM((ALTS, 4, 2, 64, 128), F32),
        pltpu.VMEM((ALTS, 4, 2, 2, 64, 128), F32),
        pltpu.VMEM((ALTS, 4, 2, 2, 64, 128), F32),
        pltpu.VMEM((ALTS, 4, 2, CH, BP), F32),
        pltpu.VMEM((ALTS, 3, 2, CH, BP), F32),
        pltpu.VMEM((ALTS, 2, 2, CH, BP), F32),
        pltpu.VMEM((ALTS, 8, 2, CH, BP), F32),
        pltpu.VMEM((ALTS, 2, 24, wide), F32),
        pltpu.VMEM((ALTS, 24, wide), F32),
        pltpu.VMEM((ALTS, NY, 24, wide), F32),
        pltpu.VMEM((ALTS, 2, 24, wide), F32),
        dma((ALTS, 6, 4)), dma((ALTS, 6, 4)),
        dma((ALTS, 15)), dma((ALTS, 15)),
        dma((ALTS, 15)), dma((ALTS, 15)),
        dma((ALTS, 4, 4)), dma((ALTS, 4, 4)),
        dma((ALTS, 5)), dma((ALTS, 5)),
    ]
    vmem = pl.BlockSpec(memory_space=pltpu.VMEM)
    theta, labt = pl.pallas_call(
        functools.partial(kernel, count, stars),
        out_shape=(
            jax.ShapeDtypeStruct((nfeat, pixels), F32),
            jax.ShapeDtypeStruct((count, stars), F32),
        ),
        in_specs=[vmem] * 10,
        out_specs=(vmem, vmem),
        scratch_shapes=scratch,
        compiler_params=pltpu.CompilerParams(
            collective_id=0, has_side_effects=True, vmem_limit_bytes=60 * 1024 * 1024
        ),
    )(flux, inv_var, coeffs, labels.T, *tables(count))
    return theta, labt.T


def solution(mesh):
    return jax.shard_map(
        per_device,
        mesh=mesh,
        in_specs=(P("star", "pix"), P("star", "pix"), P(None, "pix"), P("star", None)),
        out_specs=(P(None, "pix"), P("star", None)),
        check_vma=False,
    )
```

```python
import functools

import jax
import jax.numpy as jnp
import numpy as np
from jax import lax
from jax.experimental import pallas as pl
from jax.experimental.pallas import tpu as pltpu
from jax.sharding import PartitionSpec as P

ALTS = 2
STEP = 0.25
NX, NZ, NY = 4, 16, 4
F = 256
BP = 256
CH = 16
KL = 32
MESH = pl.DeviceIdType.MESH
BF = jnp.bfloat16
F32 = jnp.float32


def tables(count):
    left = np.full((F,), -1, np.int32)
    right = np.full((F,), -1, np.int32)
    left[0] = right[0] = count
    for m in range(count):
        left[1 + m], right[1 + m] = m, count
    pos = 1 + count
    pair = np.zeros((count, count), np.int32)
    for i in range(count):
        for j in range(i, count):
            left[pos], right[pos] = i, j
            pair[i, j] = pair[j, i] = pos
            pos += 1
    sl = np.zeros((128, F), np.float32)
    sr = np.zeros((128, F), np.float32)
    for f in range(pos):
        sl[left[f], f] = 1.0
        sr[right[f], f] = 1.0
    pick = np.zeros((count * KL, F), np.float32)
    for m in range(count):
        for j in range(count):
            pick[m * KL + j, pair[m, j]] = 2.0 if j == m else 1.0
        pick[m * KL + count, 1 + m] = 1.0
    back_l = sl.T.copy()
    back_r = sr.T.copy()
    back_l[:, count:] = 0.0
    back_r[:, count:] = 0.0
    cols = np.zeros((128, 2 * F), np.float32)
    for t in range(3):
        cols[24 * t : 24 * t + 24] = np.concatenate([sl, sr], axis=1)[:24]
    rows_l, rows_r = cols[:, :F].T, cols[:, F:].T
    twice = lambda t: np.concatenate([t, t], axis=0)
    mats = (cols, twice(rows_l), twice(rows_r), pick, twice(back_l), twice(back_r))
    return [jnp.asarray(t, BF) for t in mats]


def nn(a, b):
    return lax.dot_general(a, b, (((1,), (0,)), ((), ())), preferred_element_type=F32)


def nt(a, b):
    return lax.dot_general(a, b, (((1,), (1,)), ((), ())), preferred_element_type=F32)


def three(v):
    hi = v.astype(BF)
    rest = v - hi.astype(F32)
    mid = rest.astype(BF)
    low = (rest - mid.astype(F32)).astype(BF)
    return hi, mid, low


def kernel(
    count, stars, flux, ivar, coeffs, labels, cols, rows_l, rows_r, pick, back_l, back_r,
    theta_out, lab_out,
    th, thb, lt, colsr, pickr, fb, ftb, sqt, selh, labb, iv, ivf, w, part, xs, g_acc, tall, ac, lgc,
    xr1, xr2, zfp, zfm, zrl, zr, halves, p1, yb, fin,
    sxs, sxr, szs, szr, sas, sar, sbs, sbr, sps, spr,
):
    star = lax.axis_index("star")
    pix = lax.axis_index("pix")
    x, z = star // NZ, star % NZ
    y, core = pix // 2, pix % 2

    def star_at(dx, dz):
        return {"star": ((x + dx) % NX) * NZ + (z + dz) % NZ}

    right, left = star_at(1, 0), star_at(NX - 1, 0)
    partner = {"pix": y * 2 + 1 - core}

    def along_z(d):
        return star_at(0, d % NZ)

    def along_y(d):
        return {"pix": ((y + d) % NY) * 2 + core}

    def rcopy(src, dst, ssem, rsem, dev):
        return pltpu.make_async_remote_copy(
            src_ref=src, dst_ref=dst, send_sem=ssem, recv_sem=rsem,
            device_id=dev, device_id_type=MESH,
        )

    zpeers = (1, 2, 3, 4, -1, -2, -3, -4)
    peers = [right, left, partner] + [along_z(d) for d in zpeers] + [along_y(d) for d in (1, 2, 3)]
    barrier = pltpu.get_barrier_semaphore()
    for peer in peers:
        pl.semaphore_signal(barrier, inc=1, device_id=peer, device_id_type=MESH)

    def tile(h, b):
        return pl.ds(pl.multiple_of(h * 512 + b * 128, 128), 128)

    def block(h, j):
        return pl.ds(pl.multiple_of(h * 512 + j * 256, 256), 256)

    def pos(d):
        return CH * ((d + 3) % NZ)

    def at_row(chunk):
        return pl.ds(pl.multiple_of(((chunk - z + 3 + NZ) % NZ) * CH, CH), CH)

    first = (z + NZ - 3) % NZ
    zrot = pl.multiple_of(first * CH, CH)
    nfeat, pixels = coeffs.shape
    for c in range(NZ):
        have = min(max(nfeat - c * CH, 0), CH)
        rows = coeffs[pl.ds(c * CH, have), :] if have else jnp.zeros((CH, pixels), F32)
        if 0 < have < CH:
            rows = jnp.concatenate([rows, jnp.zeros((CH - have, pixels), F32)], axis=0)
        th[0, at_row(c), :] = rows
        thb[at_row(c), :] = rows.astype(BF)
    wide = lt.shape[1]
    lt[...] = jnp.zeros(lt.shape, F32)
    lt[pl.ds(0, count), pl.ds(0, stars)] = labels[...]
    lt[pl.ds(count, 1), pl.ds(0, stars)] = jnp.ones((1, stars), F32)
    iv[pl.ds(0, stars), :] = ivar[...]
    iv[pl.ds(stars, wide - stars), :] = jnp.zeros((wide - stars, pixels), BF)
    ivf[...] = ivar[...].astype(F32)
    w[pl.ds(stars, wide - stars), :] = jnp.zeros((wide - stars, pixels), BF)
    lgc[...] = jnp.zeros(lgc.shape, F32)
    back = (F - zrot) % F
    for h in (0, F):
        colsr[:, pl.ds(h, F)] = pltpu.roll(cols[:, pl.ds(h, F)].astype(F32), back, 1).astype(BF)
    pickr[...] = pltpu.roll(pick[...].astype(F32), back, 1).astype(BF)

    opp, rgt, lft = (x + 2) % NX, (x + 1) % NX, (x + 3) % NX
    lane = lax.broadcasted_iota(jnp.int32, (stars, 128), 1)
    zd = {1: 0, 2: 1, 3: 2, -1: 3, -2: 4, -3: 5, 4: 6, -4: 7, 5: 8, 6: 9, 7: 10, 8: 11, -5: 12, -6: 13, -7: 14}
    groups = (2, 3, 1, 0)

    def rows(k):
        return pl.ds(64 * k, 64)

    def weigh(p):
        model = nn(fb[...], thb[:, p])
        return (ivf[:, p] * (flux[:, p].astype(F32) - model)).astype(BF)

    def turn_body(turn, carry):
        hi, mid, low = three(lt[...])
        stack = jnp.concatenate(
            [hi.astype(F32), mid.astype(F32), low.astype(F32), jnp.zeros((128 - 72, wide), F32)], axis=0
        )
        stack_b = stack.astype(BF)
        stack_t = stack.T.astype(BF)
        featt = nn(rows_l[pl.ds(zrot, F), :], stack_b) * nn(rows_r[pl.ds(zrot, F), :], stack_b)
        ftb[...] = featt.astype(BF)
        sqt[...] = (featt * featt).astype(BF)
        full = nn(stack_t[:stars], colsr[...])
        fb[...] = (full[:, :F] * full[:, F:]).astype(BF)
        selh[...] = full.astype(BF)
        labb[...] = stack_t[:stars, :KL]

        def grads(p):
            part[turn, 1, :, p] = nn(sqt[...], iv[:, p])
            w[pl.ds(0, stars), p] = weigh(p)
            part[turn, 0, :, p] = nn(ftb[...], w[:, p])

        def xcopy(h, n, k):
            s, r = sxs.at[turn, h, n, k], sxr.at[turn, h, n, k]
            what, b = ((0, opp), (1, opp), (1, rgt), (0, lft), (0, rgt), (1, lft))[n]
            src = part.at[turn, what, rows(k), tile(h, b)]
            side = n % 2
            if n < 2:
                dst = xr1.at[turn, h, side, k]
            else:
                dst = xr2.at[turn, h, side, what, k]
            return rcopy(src, dst, s, r, left if side else right)

        def send_x(h, k):
            for n in range(4):
                xcopy(h, n, k).start()

        def relay_x(h, k):
            for side, what, b in ((0, 0, rgt), (1, 1, lft)):
                xcopy(h, side, k).wait_recv()
                part[turn, what, rows(k), tile(h, b)] = (
                    part[turn, what, rows(k), tile(h, b)] + xr1[turn, h, side, k]
                )
                xcopy(h, 4 + side, k).start()

        def finish_x(h, k):
            for n in (2, 3, 4, 5):
                xcopy(h, n, k).wait_recv()
            for what in (0, 1):
                xs[turn, h, what, rows(k), :] = (
                    part[turn, what, rows(k), tile(h, x)]
                    + xr2[turn, h, 0, what, k]
                    + xr2[turn, h, 1, what, k]
                )

        def chunk(h, d):
            return xs.at[turn, h, :, pl.ds(pos(d), CH), :]

        def zcopy(h, d):
            s, r = szs.at[turn, h, zd[d]], szr.at[turn, h, zd[d]]
            if d > 4:
                return rcopy(chunk(h, d), zfp.at[turn, h, d - 5], s, r, along_z(d - 4))
            if d < -4:
                return rcopy(chunk(h, d), zfm.at[turn, h, -d - 5], s, r, along_z(d + 4))
            src = chunk(h, d) if abs(d) < 4 else zrl.at[turn, h, 0 if d > 0 else 1]
            return rcopy(src, zr.at[turn, h, zd[d]], s, r, along_z(d))

        def send_z(h, ds):
            for d in ds:
                zcopy(h, d).start()

        def relay_z(h):
            for d in (8, 7, 6, 5):
                zcopy(h, d).wait_recv()
            zrl[turn, h, 0] = chunk(h, 4)[...] + (
                (zfp[turn, h, 0] + zfp[turn, h, 1]) + (zfp[turn, h, 2] + zfp[turn, h, 3])
            )
            zcopy(h, 4).start()
            for d in (-7, -6, -5):
                zcopy(h, d).wait_recv()
            zrl[turn, h, 1] = chunk(h, -4)[...] + ((zfm[turn, h, 0] + zfm[turn, h, 1]) + zfm[turn, h, 2])
            zcopy(h, -4).start()

        new = th.at[turn + 1]
        mine = pl.ds(pos(0), CH)

        def update(h):
            for d in (3, 2, 1, -3, -2, -1, 4, -4):
                zcopy(h, d).wait_recv()
            total = chunk(h, 0)[...]
            for i in range(8):
                total = total + zr[turn, h, i]
            th[turn + 1, mine, tile(h, x)] = th[turn, mine, tile(h, x)] + STEP * total[0] / (1.0 + total[1])
            for d in (4, -4, 3, -3, 2, -2, 1, -1):
                acopy(h, d).start()

        def acopy(h, d):
            s, r = sas.at[turn, h, zd[d]], sar.at[turn, h, zd[d]]
            if abs(d) <= 4:
                src, dst, hop = pos(0), pos(-d), d
            else:
                hop = d - 4 if d > 0 else d + 4
                src, dst = pos(-4 if d > 0 else 4), pos(-d)
            return rcopy(
                new.at[pl.ds(src, CH), tile(h, x)], new.at[pl.ds(dst, CH), tile(h, x)], s, r, along_z(hop)
            )

        def relay_a(h):
            acopy(h, 4).wait_recv()
            for e in (8, 7, 6, 5):
                acopy(h, e).start()
            acopy(h, -4).wait_recv()
            for e in (-7, -6, -5):
                acopy(h, e).start()

        def bcopy(h, n, k):
            s, r = sbs.at[turn, h, n, k], sbr.at[turn, h, n, k]
            if n < 2:
                ref = new.at[rows(k), tile(h, x)]
            elif n == 2:
                ref = new.at[pl.ds(64 * k, 32), tile(h, lft)]
            else:
                ref = new.at[pl.ds(64 * k + 32, 32), tile(h, rgt)]
            return rcopy(ref, ref, s, r, right if n % 2 == 0 else left)

        def spread(h, ds, k):
            for d in ds:
                acopy(h, d).wait_recv()
            bcopy(h, 0, k).start()
            bcopy(h, 1, k).start()

        def pass_on(h, k):
            bcopy(h, 0, k).wait_recv()
            bcopy(h, 2, k).start()
            bcopy(h, 1, k).wait_recv()
            bcopy(h, 3, k).start()

        def wait_far(h):
            for k in range(4):
                bcopy(h, 2, k).wait_recv()
                bcopy(h, 3, k).wait_recv()

        def label_block(h, j, place):
            p = block(h, j)
            thb[:, p] = th[turn + 1, :, p].astype(BF)
            t = thb[:, p]
            part_g = nt(weigh(p), t)
            g_acc[...] = part_g if place == 0 else g_acc[...] + part_g
            tall[...] = nn(pickr[...], t).astype(BF)

            def some(i, c):
                for u in range(4):
                    m = 4 * i + u
                    jac = nn(labb[...], tall[pl.ds(pl.multiple_of(m * KL, KL), KL), :])
                    q = ivf[:, p] * jac * jac
                    q = q[:, :128] + q[:, 128:]
                    if place > 0:
                        q = ac[m] + q
                    if place < 3:
                        ac[m] = q
                    else:
                        tot = jnp.sum(q, axis=1, keepdims=True)
                        lgc[pl.ds(0, stars), :] = jnp.where(lane == 24 + m, tot, lgc[pl.ds(0, stars), :])
                return c

            lax.fori_loop(0, count // 4, some, 0)

        near, away = x // 2, 1 - x // 2
        g0, g1, g2, g3 = groups
        far_up, far_down = (8, 7, 6, 5), (-7, -6, -5)
        grads(block(0, away))
        grads(block(0, near))

        @pl.when(turn == 0)
        def _():
            pl.semaphore_wait(barrier, len(peers))

        send_x(0, g0)
        send_x(0, g1)
        grads(block(1, away))
        relay_x(0, g0)
        send_x(0, g2)
        grads(block(1, near))
        relay_x(0, g1)
        send_x(0, g3)
        finish_x(0, g0)
        send_z(0, far_up)
        relay_x(0, g2)
        send_x(1, g0)
        send_x(1, g1)
        finish_x(0, g1)
        send_z(0, far_down)
        relay_x(0, g3)
        send_x(1, g2)
        finish_x(0, g2)
        send_z(0, (3, 2, 1))
        finish_x(0, g3)
        send_z(0, (-3, -2, -1))
        relay_x(1, g0)
        relay_z(0)
        send_x(1, g3)
        relay_x(1, g1)
        finish_x(1, g0)
        send_z(1, far_up)
        relay_x(1, g2)
        update(0)
        finish_x(1, g1)
        send_z(1, far_down)
        relay_x(1, g3)
        finish_x(1, g2)
        send_z(1, (3, 2, 1))
        finish_x(1, g3)
        send_z(1, (-3, -2, -1))
        relay_a(0)
        relay_z(1)
        spread(0, (3, 2, 1), 0)
        spread(0, (-3, -2, -1), 1)
        pass_on(0, 0)
        pass_on(0, 1)
        update(1)
        spread(0, (5, 6, 7), 3)
        spread(0, (-5, -6, -7, 8), 2)
        pass_on(0, 3)
        pass_on(0, 2)
        label_block(0, near, 0)
        relay_a(1)
        spread(1, (3, 2, 1), 0)
        spread(1, (-3, -2, -1), 1)
        wait_far(0)
        label_block(0, away, 1)
        pass_on(1, 0)
        pass_on(1, 1)
        spread(1, (5, 6, 7), 3)
        spread(1, (-5, -6, -7, 8), 2)
        pass_on(1, 3)
        pass_on(1, 2)
        label_block(1, near, 2)
        wait_far(1)
        label_block(1, away, 3)

        lg = jnp.zeros((stars, 128), F32)
        for h, table in ((selh[:, F:], back_l), (selh[:, :F], back_r)):
            h = g_acc[...] * h.astype(F32)
            h0 = h.astype(BF)
            h1 = (h - h0.astype(F32)).astype(BF)
            b = table[pl.ds(zrot, F), :]
            lg = lg + nn(h0, b) + nn(h1, b)
        low_lanes = lane < 24
        lgc[pl.ds(0, stars), :] = jnp.where(low_lanes, lg, lgc[pl.ds(0, stars), :])
        sums = lgc[...].T
        halves[turn, 0] = sums[0:24]
        halves[turn, 1] = sums[24:48]

        def pcopy(n):
            s, r = sps.at[turn, n], spr.at[turn, n]
            if n == 0:
                return rcopy(halves.at[turn, 1 - core], p1.at[turn], s, r, partner)
            if n == 4:
                ref = fin.at[turn, core]
                return rcopy(ref, ref, s, r, partner)
            ref = yb.at[turn, y]
            return rcopy(ref, ref, s, r, along_y(n))

        pcopy(0).start()
        pcopy(0).wait_recv()
        yb[turn, y] = halves[turn, core] + p1[turn]
        for n in (2, 1, 3):
            pcopy(n).start()

        @pl.when(turn == ALTS - 1)
        def _():
            for c in range(NZ):
                have = min(max(nfeat - c * CH, 0), CH)
                if have:
                    theta_out[pl.ds(c * CH, have), :] = new[at_row(c), :][:have]

        for n in (1, 2, 3):
            pcopy(n).wait_recv()
        fin[turn, core] = (yb[turn, 0] + yb[turn, 1]) + (yb[turn, 2] + yb[turn, 3])
        pcopy(4).start()
        pcopy(4).wait_recv()
        lab = lt[...]
        row = lax.broadcasted_iota(jnp.int32, lab.shape, 0)
        lt[...] = jnp.where(row < count, lab + (fin[turn, 0] - lab) / (1.0 + fin[turn, 1]), lab)

        for h in (0, 1):
            for k in groups:
                for n in range(6):
                    xcopy(h, n, k).wait_send()
                for n in range(4):
                    bcopy(h, n, k).wait_send()
            for d in zd:
                zcopy(h, d).wait_send()
                acopy(h, d).wait_send()
        for n in range(5):
            pcopy(n).wait_send()
        return carry

    lax.fori_loop(0, ALTS, turn_body, 0)
    lab_out[...] = lt[pl.ds(0, count), pl.ds(0, stars)]


def per_device(flux, inv_var, coeffs, labels):
    stars, count = labels.shape
    pixels = flux.shape[1]
    nfeat = coeffs.shape[0]
    wide = -(-stars // 128) * 128
    dma = pltpu.SemaphoreType.DMA
    scratch = [
        pltpu.VMEM((ALTS + 1, F, pixels), F32),
        pltpu.VMEM((F, pixels), BF),
        pltpu.VMEM((24, wide), F32),
        pltpu.VMEM((128, 2 * F), BF),
        pltpu.VMEM((count * KL, F), BF),
        pltpu.VMEM((stars, F), BF),
        pltpu.VMEM((F, wide), BF),
        pltpu.VMEM((F, wide), BF),
        pltpu.VMEM((stars, 2 * F), BF),
        pltpu.VMEM((stars, KL), BF),
        pltpu.VMEM((wide, pixels), BF),
        pltpu.VMEM((stars, pixels), F32),
        pltpu.VMEM((wide, pixels), BF),
        pltpu.VMEM((ALTS, 2, F, pixels), F32),
        pltpu.VMEM((ALTS, 2, 2, F, 128), F32),
        pltpu.VMEM((stars, F), F32),
        pltpu.VMEM((count * KL, BP), BF),
        pltpu.VMEM((count, stars, 128), F32),
        pltpu.VMEM((wide, 128), F32),
        pltpu.VMEM((ALTS, 2, 2, 4, 64, 128), F32),
        pltpu.VMEM((ALTS, 2, 2, 2, 4, 64, 128), F32),
        pltpu.VMEM((ALTS, 2, 4, 2, CH, 128), F32),
        pltpu.VMEM((ALTS, 2, 3, 2, CH, 128), F32),
        pltpu.VMEM((ALTS, 2, 2, 2, CH, 128), F32),
        pltpu.VMEM((ALTS, 2, 8, 2, CH, 128), F32),
        pltpu.VMEM((ALTS, 2, 24, wide), F32),
        pltpu.VMEM((ALTS, 24, wide), F32),
        pltpu.VMEM((ALTS, NY, 24, wide), F32),
        pltpu.VMEM((ALTS, 2, 24, wide), F32),
        dma((ALTS, 2, 6, 4)), dma((ALTS, 2, 6, 4)),
        dma((ALTS, 2, 15)), dma((ALTS, 2, 15)),
        dma((ALTS, 2, 15)), dma((ALTS, 2, 15)),
        dma((ALTS, 2, 4, 4)), dma((ALTS, 2, 4, 4)),
        dma((ALTS, 5)), dma((ALTS, 5)),
    ]
    vmem = pl.BlockSpec(memory_space=pltpu.VMEM)
    theta, labt = pl.pallas_call(
        functools.partial(kernel, count, stars),
        out_shape=(
            jax.ShapeDtypeStruct((nfeat, pixels), F32),
            jax.ShapeDtypeStruct((count, stars), F32),
        ),
        in_specs=[vmem] * 10,
        out_specs=(vmem, vmem),
        scratch_shapes=scratch,
        compiler_params=pltpu.CompilerParams(
            collective_id=0, has_side_effects=True, vmem_limit_bytes=60 * 1024 * 1024
        ),
    )(flux, inv_var, coeffs, labels.T, *tables(count))
    return theta, labt.T


def solution(mesh):
    return jax.shard_map(
        per_device,
        mesh=mesh,
        in_specs=(P("star", "pix"), P("star", "pix"), P(None, "pix"), P("star", None)),
        out_specs=(P(None, "pix"), P("star", None)),
        check_vma=False,
    )
```

```python
import functools

import jax
import jax.numpy as jnp
import numpy as np
from jax import lax
from jax.experimental import pallas as pl
from jax.experimental.pallas import tpu as pltpu
from jax.sharding import PartitionSpec as P

ALTS = 2
STEP = 0.25
NX, NZ, NY = 4, 16, 4
F = 256
BP = 256
CH = 16
KL = 32
MESH = pl.DeviceIdType.MESH
BF = jnp.bfloat16
F32 = jnp.float32


def tables(count):
    left = np.full((F,), -1, np.int32)
    right = np.full((F,), -1, np.int32)
    left[0] = right[0] = count
    for m in range(count):
        left[1 + m], right[1 + m] = m, count
    pos = 1 + count
    pair = np.zeros((count, count), np.int32)
    for i in range(count):
        for j in range(i, count):
            left[pos], right[pos] = i, j
            pair[i, j] = pair[j, i] = pos
            pos += 1
    sl = np.zeros((128, F), np.float32)
    sr = np.zeros((128, F), np.float32)
    for f in range(pos):
        sl[left[f], f] = 1.0
        sr[right[f], f] = 1.0
    pick = np.zeros((count * KL, F), np.float32)
    for m in range(count):
        top = (m // 2 + m % 2 * (count // 2)) * KL
        for j in range(count):
            pick[top + j, pair[m, j]] = 2.0 if j == m else 1.0
        pick[top + count, 1 + m] = 1.0
    back_l = sl.T.copy()
    back_r = sr.T.copy()
    back_l[:, count:] = 0.0
    back_r[:, count:] = 0.0
    cols = np.zeros((128, 2 * F), np.float32)
    for t in range(3):
        cols[24 * t : 24 * t + 24] = np.concatenate([sl, sr], axis=1)[:24]
    rows_l, rows_r = cols[:, :F].T, cols[:, F:].T
    twice = lambda t: np.concatenate([t, t], axis=0)
    mats = (cols, twice(rows_l), twice(rows_r), pick, twice(back_l), twice(back_r))
    return [jnp.asarray(t, BF) for t in mats]


def nn(a, b):
    return lax.dot_general(a, b, (((1,), (0,)), ((), ())), preferred_element_type=F32)


def nt(a, b):
    return lax.dot_general(a, b, (((1,), (1,)), ((), ())), preferred_element_type=F32)


def three(v):
    hi = v.astype(BF)
    rest = v - hi.astype(F32)
    mid = rest.astype(BF)
    low = (rest - mid.astype(F32)).astype(BF)
    return hi, mid, low


def kernel(
    count, stars, *refs,
):
    given, (theta_out, lab_out), held, refs = refs[:10], refs[10:12], refs[12:22], refs[22:]
    flux, ivar, coeffs, labels, cols, rows_l, rows_r, pick, back_l, back_r = held
    (
        sin, tho, th, thb, lt, colsr, pickr, fb, ftb, sqt, selh, labb, iv, ivf, w, part, xs, g_acc, tall, ac, lgc,
        xr1a, xr1b, xr2l, xr2r, zfp, zfm, zrl, zr, halves, p1, yb, fin,
        sxs, sxr, szs, szr, sas, sar, sbs, sbr, sps, spr,
    ) = refs
    star = lax.axis_index("star")
    pix = lax.axis_index("pix")
    x, z = star // NZ, star % NZ
    y, core = pix // 2, pix % 2

    def star_at(dx, dz):
        return {"star": ((x + dx) % NX) * NZ + (z + dz) % NZ}

    right, left = star_at(1, 0), star_at(NX - 1, 0)
    partner = {"pix": y * 2 + 1 - core}

    def along_z(d):
        return star_at(0, d % NZ)

    def along_y(d):
        return {"pix": ((y + d) % NY) * 2 + core}

    def rcopy(src, dst, ssem, rsem, dev):
        return pltpu.make_async_remote_copy(
            src_ref=src, dst_ref=dst, send_sem=ssem, recv_sem=rsem,
            device_id=dev, device_id_type=MESH,
        )

    zpeers = (1, 2, 3, 4, -1, -2, -3, -4)
    peers = [right, left, partner] + [along_z(d) for d in zpeers] + [along_y(d) for d in (1, 2, 3)]
    barrier = pltpu.get_barrier_semaphore()
    for peer in peers:
        pl.semaphore_signal(barrier, inc=1, device_id=peer, device_id_type=MESH)
    loads = [pltpu.make_async_copy(a, b, sin.at[i]) for i, (a, b) in enumerate(zip(given, held))]
    for i in (3, 5, 6, 4, 1, 0, 2, 7, 8, 9):
        loads[i].start()
    for i in (3, 4, 5, 6):
        loads[i].wait()

    def px(blk):
        return pl.ds(pl.multiple_of(blk * BP, BP), BP)

    def px_half(blk, half):
        return pl.ds(pl.multiple_of(blk * BP + half * 128, 128), 128)

    def pos(d):
        return CH * ((d + 3) % NZ)

    def at_row(chunk):
        return pl.ds(pl.multiple_of(((chunk - z + 3 + NZ) % NZ) * CH, CH), CH)

    first = (z + NZ - 3) % NZ
    zrot = pl.multiple_of(first * CH, CH)
    nfeat, pixels = coeffs.shape
    wide = lt.shape[1]
    lt[...] = jnp.zeros(lt.shape, F32)
    lt[pl.ds(0, count), pl.ds(0, stars)] = labels[...]
    lt[pl.ds(count, 1), pl.ds(0, stars)] = jnp.ones((1, stars), F32)
    back = (F - zrot) % F
    for h in (0, F):
        colsr[:, pl.ds(h, F)] = pltpu.roll(cols[:, pl.ds(h, F)].astype(F32), back, 1).astype(BF)

    blk_o, blk_r, blk_l = (x + 2) % NX, (x + 1) % NX, (x + 3) % NX
    lane = lax.broadcasted_iota(jnp.int32, (stars, 128), 1)
    zd = {1: 0, 2: 1, 3: 2, -1: 3, -2: 4, -3: 5, 4: 6, -4: 7, 5: 8, 6: 9, 7: 10, 8: 11, -5: 12, -6: 13, -7: 14}
    groups = range(8)

    def rows(k):
        return pl.ds(32 * k, 32)

    def weigh(blk):
        model = nn(fb[...], thb[:, px(blk)])
        return (ivf[:, px(blk)] * (flux[:, px(blk)].astype(F32) - model)).astype(BF)

    def turn_body(turn, carry):
        hi, mid, low = three(lt[...])
        stack = jnp.concatenate(
            [hi.astype(F32), mid.astype(F32), low.astype(F32), jnp.zeros((128 - 72, wide), F32)], axis=0
        )
        stack_b = stack.astype(BF)
        stack_t = stack.T.astype(BF)
        featt = nn(rows_l[pl.ds(zrot, F), :], stack_b) * nn(rows_r[pl.ds(zrot, F), :], stack_b)
        ftb[...] = featt.astype(BF)
        sqt[...] = (featt * featt).astype(BF)
        full = nn(stack_t[:stars], colsr[...])
        fb[...] = (full[:, :F] * full[:, F:]).astype(BF)
        selh[...] = full.astype(BF)
        labb[...] = stack_t[:stars, :KL]

        def grads(blk):
            part[turn, 1, :, px(blk)] = nn(sqt[...], iv[:, px(blk)])
            w[pl.ds(0, stars), px(blk)] = weigh(blk)
            part[turn, 0, :, px(blk)] = nn(ftb[...], w[:, px(blk)])

        def xcopy(n, k):
            src = part.at[turn]
            s, r = sxs.at[turn, n, k], sxr.at[turn, n, k]
            if n == 0:
                return rcopy(src.at[:, rows(k), px_half(blk_o, 0)], xr1a.at[turn, k], s, r, right)
            if n == 1:
                return rcopy(src.at[:, rows(k), px_half(blk_o, 1)], xr1b.at[turn, k], s, r, left)
            if n == 2:
                return rcopy(src.at[:, rows(k), px_half(blk_r, 1)], xr2l.at[turn, k, 1], s, r, right)
            if n == 3:
                return rcopy(src.at[:, rows(k), px_half(blk_l, 0)], xr2r.at[turn, k, 0], s, r, left)
            if n == 4:
                return rcopy(src.at[:, rows(k), px_half(blk_r, 0)], xr2l.at[turn, k, 0], s, r, right)
            return rcopy(src.at[:, rows(k), px_half(blk_l, 1)], xr2r.at[turn, k, 1], s, r, left)

        def send_x(k, pair):
            xcopy(pair, k).start()
            xcopy(pair + 1, k).start()

        def relay_x(k):
            xcopy(0, k).wait_recv()
            a = px_half(blk_r, 0)
            part[turn, :, rows(k), a] = part[turn, :, rows(k), a] + xr1a[turn, k]
            xcopy(4, k).start()
            xcopy(1, k).wait_recv()
            b = px_half(blk_l, 1)
            part[turn, :, rows(k), b] = part[turn, :, rows(k), b] + xr1b[turn, k]
            xcopy(5, k).start()

        def finish_x(k):
            for n in (2, 3, 4, 5):
                xcopy(n, k).wait_recv()
            for h in (0, 1):
                xs[turn, :, rows(k), pl.ds(128 * h, 128)] = (
                    part[turn, :, rows(k), px_half(x, h)] + xr2l[turn, k, h] + xr2r[turn, k, h]
                )

        def chunk(d):
            return xs.at[turn, :, pl.ds(pos(d), CH), :]

        def zcopy(d):
            s, r = szs.at[turn, zd[d]], szr.at[turn, zd[d]]
            if d > 4:
                return rcopy(chunk(d), zfp.at[turn, d - 5], s, r, along_z(d - 4))
            if d < -4:
                return rcopy(chunk(d), zfm.at[turn, -d - 5], s, r, along_z(d + 4))
            src = chunk(d) if abs(d) < 4 else zrl.at[turn, 0 if d > 0 else 1]
            return rcopy(src, zr.at[turn, zd[d]], s, r, along_z(d))

        @pl.when(turn == 0)
        def _():
            for i in (1, 0, 2):
                loads[i].wait()
            iv[pl.ds(0, stars), :] = ivar[...]
            iv[pl.ds(stars, wide - stars), :] = jnp.zeros((wide - stars, pixels), BF)
            ivf[...] = ivar[...].astype(F32)
            w[pl.ds(stars, wide - stars), :] = jnp.zeros((wide - stars, pixels), BF)
            for c in range(NZ):
                have = min(max(nfeat - c * CH, 0), CH)
                rows = coeffs[pl.ds(c * CH, have), :] if have else jnp.zeros((CH, pixels), F32)
                if 0 < have < CH:
                    rows = jnp.concatenate([rows, jnp.zeros((CH - have, pixels), F32)], axis=0)
                th[0, at_row(c), :] = rows
                thb[at_row(c), :] = rows.astype(BF)

        grads(blk_o)

        @pl.when(turn == 0)
        def _():
            pl.semaphore_wait(barrier, len(peers))

        def send_z(*ds):
            for d in ds:
                zcopy(d).start()

        def relay_z_up():
            for d in (8, 7, 6, 5):
                zcopy(d).wait_recv()
            zrl[turn, 0] = chunk(4)[...] + ((zfp[turn, 0] + zfp[turn, 1]) + (zfp[turn, 2] + zfp[turn, 3]))
            zcopy(4).start()

        def relay_z_down():
            for d in (-7, -6, -5):
                zcopy(d).wait_recv()
            zrl[turn, 1] = chunk(-4)[...] + ((zfm[turn, 0] + zfm[turn, 1]) + zfm[turn, 2])
            zcopy(-4).start()

        order = (5, 4, 6, 7, 3, 0, 2, 1)
        send_x(order[0], 0)
        grads(blk_r)
        grads(blk_l)
        send_x(order[0], 2)
        send_x(order[1], 0)
        send_x(order[1], 2)
        for i, k in enumerate(order):
            relay_x(k)
            if i + 2 < 8:
                send_x(order[i + 2], 0)
                send_x(order[i + 2], 2)
            if i == 0:
                grads(x)

                @pl.when(turn == 0)
                def _():
                    for j in (7, 8, 9):
                        loads[j].wait()
                    pickr[...] = pltpu.roll(pick[...].astype(F32), back, 1).astype(BF)
                    lgc[...] = jnp.zeros(lgc.shape, F32)
            if i > 0:
                finish_x(order[i - 1])
                if i == 1:
                    send_z(8, 7)
                elif i == 2:
                    send_z(6, 5)
                elif i == 3:
                    send_z(-7, -6)
                elif i == 4:
                    send_z(-5)
                elif i == 5:
                    relay_z_up()
                    send_z(3)
                elif i == 6:
                    relay_z_down()
                    send_z(-3, -2)
                elif i == 7:
                    send_z(2, 1)
        finish_x(order[7])
        send_z(-1)
        for d in (3, 2, 1, -3, -2, -1, 4, -4):
            zcopy(d).wait_recv()
        total = chunk(0)[...]
        for i in range(8):
            total = total + zr[turn, i]
        mine = pl.ds(pos(0), CH)
        th[turn + 1, mine, px(x)] = th[turn, mine, px(x)] + STEP * total[0] / (1.0 + total[1])

        new = th.at[turn + 1]

        def acopy(d):
            s, r = sas.at[turn, zd[d]], sar.at[turn, zd[d]]
            if abs(d) <= 4:
                src, dst, hop = pos(0), pos(-d), d
            else:
                hop = d - 4 if d > 0 else d + 4
                src, dst = pos(-4 if d > 0 else 4), pos(-d)
            return rcopy(
                new.at[pl.ds(src, CH), px(x)], new.at[pl.ds(dst, CH), px(x)], s, r, along_z(hop)
            )

        def part_rows(k):
            return pl.ds(pos(0), CH) if k == 8 else pl.ds(pos(-1), CH) if k == 1 else rows(k)

        def bcopy(n, k):
            s, r = sbs.at[turn, n, k], sbr.at[turn, n, k]
            at = (px(x), px(x), px_half(blk_l, 0), px_half(blk_r, 1))[n]
            ref = new.at[part_rows(k), at]
            return rcopy(ref, ref, s, r, right if n % 2 == 0 else left)

        def spread(k):
            bcopy(0, k).start()
            bcopy(1, k).start()

        def pass_on(k):
            bcopy(0, k).wait_recv()
            bcopy(2, k).start()
            bcopy(1, k).wait_recv()
            bcopy(3, k).start()

        def arrived(*ds):
            for d in ds:
                acopy(d).wait_recv()

        for d in (4, -4, 1, -1):
            acopy(d).start()
        spread(8)
        arrived(1)
        spread(1)
        for d in (2, -2, 3, -3):
            acopy(d).start()
        pass_on(8)
        arrived(4)
        for e in (8, 7, 6, 5):
            acopy(e).start()
        arrived(-4)
        for e in (-7, -6, -5):
            acopy(e).start()
        arrived(-1, -2)
        spread(2)
        arrived(3, 2)
        spread(0)
        arrived(-3)
        spread(3)
        pass_on(1)
        pass_on(2)
        arrived(5)
        spread(7)
        arrived(-5, -6)
        spread(4)
        pass_on(0)
        pass_on(3)
        arrived(6, 7)
        spread(6)
        arrived(-7, 8)
        spread(5)

        def label_block(blk, place):
            thb[:, px(blk)] = th[turn + 1, :, px(blk)].astype(BF)
            t = thb[:, px(blk)]
            part_g = nt(weigh(blk), t)
            g_acc[...] = part_g if place == 0 else g_acc[...] + part_g
            many = count // 2 * KL
            tall[:, :BP] = nn(pickr[:many], t).astype(BF)
            tall[:, BP:] = nn(pickr[many:], t).astype(BF)

            def some(i, c):
                for u in range(2):
                    pair = 2 * i + u
                    jac = nn(labb[...], tall[pl.ds(pl.multiple_of(pair * KL, KL), KL), :])
                    for v in (0, 1):
                        m = 2 * pair + v
                        j = jac[:, BP * v : BP * v + BP]
                        q = ivf[:, px(blk)] * j * j
                        q = q[:, :128] + q[:, 128:]
                        if place > 0:
                            q = ac[m] + q
                        if place < 3:
                            ac[m] = q
                        else:
                            tot = jnp.sum(q, axis=1, keepdims=True)
                            lgc[pl.ds(0, stars), :] = jnp.where(
                                lane == 24 + m, tot, lgc[pl.ds(0, stars), :]
                            )
                return c

            lax.fori_loop(0, count // 4, some, 0)

        label_block(x, 0)
        for k in (7, 4, 6, 5):
            pass_on(k)
        label_block(blk_l, 1)
        label_block(blk_r, 2)
        for k in range(9):
            bcopy(2, k).wait_recv()
            bcopy(3, k).wait_recv()
        label_block(blk_o, 3)

        lg = jnp.zeros((stars, 128), F32)
        for h, table in ((selh[:, F:], back_l), (selh[:, :F], back_r)):
            h = g_acc[...] * h.astype(F32)
            h0 = h.astype(BF)
            h1 = (h - h0.astype(F32)).astype(BF)
            b = table[pl.ds(zrot, F), :]
            lg = lg + nn(h0, b) + nn(h1, b)
        low_lanes = lane < 24
        lgc[pl.ds(0, stars), :] = jnp.where(low_lanes, lg, lgc[pl.ds(0, stars), :])
        sums = lgc[...].T
        halves[turn, 0] = sums[0:24]
        halves[turn, 1] = sums[24:48]

        def pcopy(n):
            s, r = sps.at[turn, n], spr.at[turn, n]
            if n == 0:
                return rcopy(halves.at[turn, 1 - core], p1.at[turn], s, r, partner)
            if n == 4:
                ref = fin.at[turn, core]
                return rcopy(ref, ref, s, r, partner)
            ref = yb.at[turn, y]
            return rcopy(ref, ref, s, r, along_y(n))

        pcopy(0).start()
        pcopy(0).wait_recv()
        yb[turn, y] = halves[turn, core] + p1[turn]
        for n in (2, 1, 3):
            pcopy(n).start()

        @pl.when(turn == ALTS - 1)
        def _():
            for c in range(NZ):
                have = min(max(nfeat - c * CH, 0), CH)
                if have:
                    tho[pl.ds(c * CH, have), :] = new[at_row(c), :][:have]
            save.start()

        for n in (1, 2, 3):
            pcopy(n).wait_recv()
        fin[turn, core] = (yb[turn, 0] + yb[turn, 1]) + (yb[turn, 2] + yb[turn, 3])
        pcopy(4).start()
        pcopy(4).wait_recv()
        lab = lt[...]
        row = lax.broadcasted_iota(jnp.int32, lab.shape, 0)
        lt[...] = jnp.where(row < count, lab + (fin[turn, 0] - lab) / (1.0 + fin[turn, 1]), lab)

        for k in groups:
            for n in range(6):
                xcopy(n, k).wait_send()
        for k in range(9):
            for n in range(4):
                bcopy(n, k).wait_send()
        for d in zd:
            zcopy(d).wait_send()
            acopy(d).wait_send()
        for n in range(5):
            pcopy(n).wait_send()
        return carry

    save = pltpu.make_async_copy(tho, theta_out, sin.at[10])
    lax.fori_loop(0, ALTS, turn_body, 0)
    save.wait()
    lab_out[...] = lt[pl.ds(0, count), pl.ds(0, stars)]


def hand_over(pieces, theta, lab, theta_out, lab_out, held, held_lab, ins, outs):
    rows = [pl.ds(lo, size) for lo, size in pieces]
    into = [pltpu.make_async_copy(theta.at[r], held.at[r], ins.at[i]) for i, r in enumerate(rows)]
    away = [pltpu.make_async_copy(held.at[r], theta_out.at[r], outs.at[i]) for i, r in enumerate(rows)]
    into.append(pltpu.make_async_copy(lab, held_lab, ins.at[len(rows)]))
    away.append(pltpu.make_async_copy(held_lab, lab_out, outs.at[len(rows)]))
    for copy in into:
        copy.start()
    for done, copy in zip(into, away):
        done.wait()
        copy.start()
    for copy in away:
        copy.wait()


def per_device(flux, inv_var, coeffs, labels):
    stars, count = labels.shape
    pixels = flux.shape[1]
    nfeat = coeffs.shape[0]
    wide = -(-stars // 128) * 128
    dma = pltpu.SemaphoreType.DMA
    given = (flux, inv_var, coeffs, labels.T, *tables(count))
    scratch = [
        *[pltpu.VMEM(a.shape, a.dtype) for a in given],
        dma((11,)),
        pltpu.VMEM((nfeat, pixels), F32),
        pltpu.VMEM((ALTS + 1, F, pixels), F32),
        pltpu.VMEM((F, pixels), BF),
        pltpu.VMEM((24, wide), F32),
        pltpu.VMEM((128, 2 * F), BF),
        pltpu.VMEM((count * KL, F), BF),
        pltpu.VMEM((stars, F), BF),
        pltpu.VMEM((F, wide), BF),
        pltpu.VMEM((F, wide), BF),
        pltpu.VMEM((stars, 2 * F), BF),
        pltpu.VMEM((stars, KL), BF),
        pltpu.VMEM((wide, pixels), BF),
        pltpu.VMEM((stars, pixels), F32),
        pltpu.VMEM((wide, pixels), BF),
        pltpu.VMEM((ALTS, 2, F, pixels), F32),
        pltpu.VMEM((ALTS, 2, F, BP), F32),
        pltpu.VMEM((stars, F), F32),
        pltpu.VMEM((count // 2 * KL, 2 * BP), BF),
        pltpu.VMEM((count, stars, 128), F32),
        pltpu.VMEM((wide, 128), F32),
        pltpu.VMEM((ALTS, 8, 2, 32, 128), F32),
        pltpu.VMEM((ALTS, 8, 2, 32, 128), F32),
        pltpu.VMEM((ALTS, 8, 2, 2, 32, 128), F32),
        pltpu.VMEM((ALTS, 8, 2, 2, 32, 128), F32),
        pltpu.VMEM((ALTS, 4, 2, CH, BP), F32),
        pltpu.VMEM((ALTS, 3, 2, CH, BP), F32),
        pltpu.VMEM((ALTS, 2, 2, CH, BP), F32),
        pltpu.VMEM((ALTS, 8, 2, CH, BP), F32),
        pltpu.VMEM((ALTS, 2, 24, wide), F32),
        pltpu.VMEM((ALTS, 24, wide), F32),
        pltpu.VMEM((ALTS, NY, 24, wide), F32),
        pltpu.VMEM((ALTS, 2, 24, wide), F32),
        dma((ALTS, 6, 8)), dma((ALTS, 6, 8)),
        dma((ALTS, 15)), dma((ALTS, 15)),
        dma((ALTS, 15)), dma((ALTS, 15)),
        dma((ALTS, 4, 9)), dma((ALTS, 4, 9)),
        dma((ALTS, 5)), dma((ALTS, 5)),
    ]
    vmem = pl.BlockSpec(memory_space=pltpu.VMEM)
    theta, labt = pl.pallas_call(
        functools.partial(kernel, count, stars),
        out_shape=(
            jax.ShapeDtypeStruct((nfeat, pixels), F32),
            jax.ShapeDtypeStruct((count, stars), F32),
        ),
        in_specs=[pl.BlockSpec(memory_space=pl.ANY)] * 10,
        out_specs=(pl.BlockSpec(memory_space=pl.ANY), vmem),
        scratch_shapes=scratch,
        compiler_params=pltpu.CompilerParams(
            collective_id=0, has_side_effects=True, vmem_limit_bytes=60 * 1024 * 1024
        ),
    )(*given)
    cut = [0, 64, 128, 192, nfeat]
    pieces = [(lo, hi - lo) for lo, hi in zip(cut, cut[1:])]
    hbm = pl.BlockSpec(memory_space=pl.ANY)
    theta, labt = pl.pallas_call(
        functools.partial(hand_over, pieces),
        out_shape=(
            jax.ShapeDtypeStruct(theta.shape, F32),
            jax.ShapeDtypeStruct(labt.shape, F32),
        ),
        in_specs=[hbm, hbm],
        out_specs=(hbm, hbm),
        scratch_shapes=[
            pltpu.VMEM(theta.shape, F32),
            pltpu.VMEM(labt.shape, F32),
            dma((len(pieces) + 1,)),
            dma((len(pieces) + 1,)),
        ],
    )(theta, labt)
    return theta, labt.T


def solution(mesh):
    return jax.shard_map(
        per_device,
        mesh=mesh,
        in_specs=(P("star", "pix"), P("star", "pix"), P(None, "pix"), P("star", None)),
        out_specs=(P(None, "pix"), P("star", None)),
        check_vma=False,
    )
```

```python
import functools

import jax
import jax.numpy as jnp
import numpy as np
from jax import lax
from jax.experimental import pallas as pl
from jax.experimental.pallas import tpu as pltpu
from jax.sharding import PartitionSpec as P

ALTS = 2
STEP = 0.25
NX, NZ, NY = 4, 16, 4
F = 256
BP = 256
CH = 16
KL = 32
MESH = pl.DeviceIdType.MESH
BF = jnp.bfloat16
F32 = jnp.float32


def tables(count):
    left = np.full((F,), -1, np.int32)
    right = np.full((F,), -1, np.int32)
    left[0] = right[0] = count
    for m in range(count):
        left[1 + m], right[1 + m] = m, count
    pos = 1 + count
    pair = np.zeros((count, count), np.int32)
    for i in range(count):
        for j in range(i, count):
            left[pos], right[pos] = i, j
            pair[i, j] = pair[j, i] = pos
            pos += 1
    sl = np.zeros((128, F), np.float32)
    sr = np.zeros((128, F), np.float32)
    for f in range(pos):
        sl[left[f], f] = 1.0
        sr[right[f], f] = 1.0
    pick = np.zeros((count * KL, F), np.float32)
    for m in range(count):
        top = (m // 2 + m % 2 * (count // 2)) * KL
        for j in range(count):
            pick[top + j, pair[m, j]] = 2.0 if j == m else 1.0
        pick[top + count, 1 + m] = 1.0
    back_l = sl.T.copy()
    back_r = sr.T.copy()
    back_l[:, count:] = 0.0
    back_r[:, count:] = 0.0
    cols = np.zeros((128, 2 * F), np.float32)
    for t in range(3):
        cols[24 * t : 24 * t + 24] = np.concatenate([sl, sr], axis=1)[:24]
    rows_l, rows_r = cols[:, :F].T, cols[:, F:].T
    twice = lambda t: np.concatenate([t, t], axis=0)
    mats = (cols, twice(rows_l), twice(rows_r), pick, twice(back_l), twice(back_r))
    return [jnp.asarray(t, BF) for t in mats]


def nn(a, b):
    return lax.dot_general(a, b, (((1,), (0,)), ((), ())), preferred_element_type=F32)


def nt(a, b):
    return lax.dot_general(a, b, (((1,), (1,)), ((), ())), preferred_element_type=F32)


def three(v):
    hi = v.astype(BF)
    rest = v - hi.astype(F32)
    mid = rest.astype(BF)
    low = (rest - mid.astype(F32)).astype(BF)
    return hi, mid, low


def kernel(
    count, stars, *refs,
):
    given, (theta_out, lab_out), held, refs = refs[:10], refs[10:12], refs[12:22], refs[22:]
    flux, ivar, coeffs, labels, cols, rows_l, rows_r, pick, back_l, back_r = held
    (
        sin, tho, th, thb, lt, colsr, pickr, fb, ftb, sqt, selh, labb, iv, ivf, w, part, xs, g_acc, tall, ac, lgc,
        xr1a, xr1b, xr2l, xr2r, zfp, zfm, zrl, zr, halves, p1, yb, fin,
        sxs, sxr, szs, szr, sas, sar, sbs, sbr, sps, spr,
    ) = refs
    star = lax.axis_index("star")
    pix = lax.axis_index("pix")
    x, z = star // NZ, star % NZ
    y, core = pix // 2, pix % 2

    def star_at(dx, dz):
        return {"star": ((x + dx) % NX) * NZ + (z + dz) % NZ}

    right, left = star_at(1, 0), star_at(NX - 1, 0)
    partner = {"pix": y * 2 + 1 - core}

    def along_z(d):
        return star_at(0, d % NZ)

    def along_y(d):
        return {"pix": ((y + d) % NY) * 2 + core}

    def rcopy(src, dst, ssem, rsem, dev):
        return pltpu.make_async_remote_copy(
            src_ref=src, dst_ref=dst, send_sem=ssem, recv_sem=rsem,
            device_id=dev, device_id_type=MESH,
        )

    zpeers = (1, 2, 3, 4, -1, -2, -3, -4)
    peers = [right, left, partner] + [along_z(d) for d in zpeers] + [along_y(d) for d in (1, 2, 3)]
    barrier = pltpu.get_barrier_semaphore()
    for peer in peers:
        pl.semaphore_signal(barrier, inc=1, device_id=peer, device_id_type=MESH)
    loads = [pltpu.make_async_copy(a, b, sin.at[i]) for i, (a, b) in enumerate(zip(given, held))]
    for i in (3, 5, 6, 4, 1, 0, 2, 7, 8, 9):
        loads[i].start()
    for i in (3, 4, 5, 6):
        loads[i].wait()

    def px(blk):
        return pl.ds(pl.multiple_of(blk * BP, BP), BP)

    def px_half(blk, half):
        return pl.ds(pl.multiple_of(blk * BP + half * 128, 128), 128)

    def pos(d):
        return CH * ((d + 3) % NZ)

    def at_row(chunk):
        return pl.ds(pl.multiple_of(((chunk - z + 3 + NZ) % NZ) * CH, CH), CH)

    first = (z + NZ - 3) % NZ
    zrot = pl.multiple_of(first * CH, CH)
    nfeat, pixels = coeffs.shape
    wide = lt.shape[1]
    lt[...] = jnp.zeros(lt.shape, F32)
    lt[pl.ds(0, count), pl.ds(0, stars)] = labels[...]
    lt[pl.ds(count, 1), pl.ds(0, stars)] = jnp.ones((1, stars), F32)
    back = (F - zrot) % F
    for h in (0, F):
        colsr[:, pl.ds(h, F)] = pltpu.roll(cols[:, pl.ds(h, F)].astype(F32), back, 1).astype(BF)

    blk_o, blk_r, blk_l = (x + 2) % NX, (x + 1) % NX, (x + 3) % NX
    lane = lax.broadcasted_iota(jnp.int32, (stars, 128), 1)
    zd = {1: 0, 2: 1, 3: 2, -1: 3, -2: 4, -3: 5, 4: 6, -4: 7, 5: 8, 6: 9, 7: 10, 8: 11, -5: 12, -6: 13, -7: 14}
    groups = range(8)

    def rows(k):
        return pl.ds(32 * k, 32)

    def weigh(blk):
        model = nn(fb[...], thb[:, px(blk)])
        return (ivf[:, px(blk)] * (flux[:, px(blk)].astype(F32) - model)).astype(BF)

    def turn_body(turn, carry):
        hi, mid, low = three(lt[...])
        stack = jnp.concatenate(
            [hi.astype(F32), mid.astype(F32), low.astype(F32), jnp.zeros((128 - 72, wide), F32)], axis=0
        )
        stack_b = stack.astype(BF)
        stack_t = stack.T.astype(BF)
        featt = nn(rows_l[pl.ds(zrot, F), :], stack_b) * nn(rows_r[pl.ds(zrot, F), :], stack_b)
        ftb[...] = featt.astype(BF)
        sqt[...] = (featt * featt).astype(BF)
        full = nn(stack_t[:stars], colsr[...])
        fb[...] = (full[:, :F] * full[:, F:]).astype(BF)
        selh[...] = full.astype(BF)
        labb[...] = stack_t[:stars, :KL]

        def grads(blk):
            part[turn, 1, :, px(blk)] = nn(sqt[...], iv[:, px(blk)])
            w[pl.ds(0, stars), px(blk)] = weigh(blk)
            part[turn, 0, :, px(blk)] = nn(ftb[...], w[:, px(blk)])

        def xcopy(n, k):
            src = part.at[turn]
            s, r = sxs.at[turn, n, k], sxr.at[turn, n, k]
            if n == 0:
                return rcopy(src.at[:, rows(k), px_half(blk_o, 0)], xr1a.at[turn, k], s, r, right)
            if n == 1:
                return rcopy(src.at[:, rows(k), px_half(blk_o, 1)], xr1b.at[turn, k], s, r, left)
            if n == 2:
                return rcopy(src.at[:, rows(k), px_half(blk_r, 1)], xr2l.at[turn, k, 1], s, r, right)
            if n == 3:
                return rcopy(src.at[:, rows(k), px_half(blk_l, 0)], xr2r.at[turn, k, 0], s, r, left)
            if n == 4:
                return rcopy(src.at[:, rows(k), px_half(blk_r, 0)], xr2l.at[turn, k, 0], s, r, right)
            return rcopy(src.at[:, rows(k), px_half(blk_l, 1)], xr2r.at[turn, k, 1], s, r, left)

        def send_x(k, pair):
            xcopy(pair, k).start()
            xcopy(pair + 1, k).start()

        def relay_x(k):
            xcopy(0, k).wait_recv()
            a = px_half(blk_r, 0)
            part[turn, :, rows(k), a] = part[turn, :, rows(k), a] + xr1a[turn, k]
            xcopy(4, k).start()
            xcopy(1, k).wait_recv()
            b = px_half(blk_l, 1)
            part[turn, :, rows(k), b] = part[turn, :, rows(k), b] + xr1b[turn, k]
            xcopy(5, k).start()

        def finish_x(k):
            for n in (2, 3, 4, 5):
                xcopy(n, k).wait_recv()
            for h in (0, 1):
                xs[turn, :, rows(k), pl.ds(128 * h, 128)] = (
                    part[turn, :, rows(k), px_half(x, h)] + xr2l[turn, k, h] + xr2r[turn, k, h]
                )

        def chunk(d):
            return xs.at[turn, :, pl.ds(pos(d), CH), :]

        def zcopy(d):
            s, r = szs.at[turn, zd[d]], szr.at[turn, zd[d]]
            if d > 4:
                return rcopy(chunk(d), zfp.at[turn, d - 5], s, r, along_z(d - 4))
            if d < -4:
                return rcopy(chunk(d), zfm.at[turn, -d - 5], s, r, along_z(d + 4))
            src = chunk(d) if abs(d) < 4 else zrl.at[turn, 0 if d > 0 else 1]
            return rcopy(src, zr.at[turn, zd[d]], s, r, along_z(d))

        @pl.when(turn == 0)
        def _():
            for i in (1, 0, 2):
                loads[i].wait()
            iv[pl.ds(0, stars), :] = ivar[...]
            iv[pl.ds(stars, wide - stars), :] = jnp.zeros((wide - stars, pixels), BF)
            ivf[...] = ivar[...].astype(F32)
            w[pl.ds(stars, wide - stars), :] = jnp.zeros((wide - stars, pixels), BF)
            for c in range(NZ):
                have = min(max(nfeat - c * CH, 0), CH)
                rows = coeffs[pl.ds(c * CH, have), :] if have else jnp.zeros((CH, pixels), F32)
                if 0 < have < CH:
                    rows = jnp.concatenate([rows, jnp.zeros((CH - have, pixels), F32)], axis=0)
                th[0, at_row(c), :] = rows
                thb[at_row(c), :] = rows.astype(BF)

        grads(blk_o)

        @pl.when(turn == 0)
        def _():
            pl.semaphore_wait(barrier, len(peers))

        def send_z(*ds):
            for d in ds:
                zcopy(d).start()

        def relay_z_up():
            for d in (8, 7, 6, 5):
                zcopy(d).wait_recv()
            zrl[turn, 0] = chunk(4)[...] + ((zfp[turn, 0] + zfp[turn, 1]) + (zfp[turn, 2] + zfp[turn, 3]))
            zcopy(4).start()

        def relay_z_down():
            for d in (-7, -6, -5):
                zcopy(d).wait_recv()
            zrl[turn, 1] = chunk(-4)[...] + ((zfm[turn, 0] + zfm[turn, 1]) + zfm[turn, 2])
            zcopy(-4).start()

        order = (5, 4, 6, 7, 3, 0, 2, 1)
        send_x(order[0], 0)
        grads(blk_r)
        grads(blk_l)
        send_x(order[0], 2)
        send_x(order[1], 0)
        send_x(order[1], 2)
        for i, k in enumerate(order):
            relay_x(k)
            if i + 2 < 8:
                send_x(order[i + 2], 0)
                send_x(order[i + 2], 2)
            if i == 0:
                grads(x)

                @pl.when(turn == 0)
                def _():
                    for j in (7, 8, 9):
                        loads[j].wait()
                    pickr[...] = pltpu.roll(pick[...].astype(F32), back, 1).astype(BF)
                    lgc[...] = jnp.zeros(lgc.shape, F32)
            if i > 0:
                finish_x(order[i - 1])
                if i == 1:
                    send_z(8, 7)
                elif i == 2:
                    send_z(6, 5)
                elif i == 3:
                    send_z(-7, -6)
                elif i == 4:
                    send_z(-5)
                elif i == 5:
                    relay_z_up()
                    send_z(3)
                elif i == 6:
                    relay_z_down()
                    send_z(-3, -2)
                elif i == 7:
                    send_z(2, 1)
        finish_x(order[7])
        send_z(-1)
        for d in (3, 2, 1, -3, -2, -1, 4, -4):
            zcopy(d).wait_recv()
        total = chunk(0)[...]
        for i in range(8):
            total = total + zr[turn, i]
        mine = pl.ds(pos(0), CH)
        th[turn + 1, mine, px(x)] = th[turn, mine, px(x)] + STEP * total[0] / (1.0 + total[1])

        new = th.at[turn + 1]

        def acopy(d):
            s, r = sas.at[turn, zd[d]], sar.at[turn, zd[d]]
            if abs(d) <= 4:
                src, dst, hop = pos(0), pos(-d), d
            else:
                hop = d - 4 if d > 0 else d + 4
                src, dst = pos(-4 if d > 0 else 4), pos(-d)
            return rcopy(
                new.at[pl.ds(src, CH), px(x)], new.at[pl.ds(dst, CH), px(x)], s, r, along_z(hop)
            )

        def part_rows(k):
            return pl.ds(pos(0), CH) if k == 8 else pl.ds(pos(-1), CH) if k == 1 else rows(k)

        def bcopy(n, k):
            s, r = sbs.at[turn, n, k], sbr.at[turn, n, k]
            at = (px(x), px(x), px_half(blk_l, 0), px_half(blk_r, 1))[n]
            ref = new.at[part_rows(k), at]
            return rcopy(ref, ref, s, r, right if n % 2 == 0 else left)

        def spread(k):
            bcopy(0, k).start()
            bcopy(1, k).start()

        def pass_on(k):
            bcopy(0, k).wait_recv()
            bcopy(2, k).start()
            bcopy(1, k).wait_recv()
            bcopy(3, k).start()

        def arrived(*ds):
            for d in ds:
                acopy(d).wait_recv()

        for d in (4, -4, 1, -1, 2, -2, 3, -3):
            acopy(d).start()
        spread(8)
        arrived(1)
        spread(1)
        pass_on(8)
        arrived(4)
        for e in (8, 7, 6, 5):
            acopy(e).start()
        arrived(-4)
        for e in (-7, -6, -5):
            acopy(e).start()
        arrived(-1, -2)
        spread(2)
        arrived(3, 2)
        spread(0)
        arrived(-3)
        spread(3)
        pass_on(1)
        pass_on(2)
        arrived(5)
        spread(7)
        arrived(-5, -6)
        spread(4)
        pass_on(0)
        pass_on(3)
        arrived(6, 7)
        spread(6)
        arrived(-7, 8)
        spread(5)

        def label_block(blk, place):
            thb[:, px(blk)] = th[turn + 1, :, px(blk)].astype(BF)
            t = thb[:, px(blk)]
            part_g = nt(weigh(blk), t)
            g_acc[...] = part_g if place == 0 else g_acc[...] + part_g
            many = count // 2 * KL
            tall[:, :BP] = nn(pickr[:many], t).astype(BF)
            tall[:, BP:] = nn(pickr[many:], t).astype(BF)

            def some(i, c):
                for u in range(2):
                    pair = 2 * i + u
                    jac = nn(labb[...], tall[pl.ds(pl.multiple_of(pair * KL, KL), KL), :])
                    for v in (0, 1):
                        m = 2 * pair + v
                        j = jac[:, BP * v : BP * v + BP]
                        q = ivf[:, px(blk)] * j * j
                        q = q[:, :128] + q[:, 128:]
                        if place > 0:
                            q = ac[m] + q
                        if place < 3:
                            ac[m] = q
                        else:
                            tot = jnp.sum(q, axis=1, keepdims=True)
                            lgc[pl.ds(0, stars), :] = jnp.where(
                                lane == 24 + m, tot, lgc[pl.ds(0, stars), :]
                            )
                return c

            lax.fori_loop(0, count // 4, some, 0)

        label_block(x, 0)
        for k in (7, 4, 6, 5):
            pass_on(k)
        label_block(blk_l, 1)
        label_block(blk_r, 2)
        for k in range(9):
            bcopy(2, k).wait_recv()
            bcopy(3, k).wait_recv()
        label_block(blk_o, 3)

        lg = jnp.zeros((stars, 128), F32)
        for h, table in ((selh[:, F:], back_l), (selh[:, :F], back_r)):
            h = g_acc[...] * h.astype(F32)
            h0 = h.astype(BF)
            h1 = (h - h0.astype(F32)).astype(BF)
            b = table[pl.ds(zrot, F), :]
            lg = lg + nn(h0, b) + nn(h1, b)
        low_lanes = lane < 24
        lgc[pl.ds(0, stars), :] = jnp.where(low_lanes, lg, lgc[pl.ds(0, stars), :])
        sums = lgc[...].T
        halves[turn, 0] = sums[0:24]
        halves[turn, 1] = sums[24:48]

        def pcopy(n):
            s, r = sps.at[turn, n], spr.at[turn, n]
            if n == 0:
                return rcopy(halves.at[turn, 1 - core], p1.at[turn], s, r, partner)
            if n == 4:
                ref = fin.at[turn, core]
                return rcopy(ref, ref, s, r, partner)
            ref = yb.at[turn, y]
            return rcopy(ref, ref, s, r, along_y(n))

        pcopy(0).start()
        pcopy(0).wait_recv()
        yb[turn, y] = halves[turn, core] + p1[turn]
        for n in (2, 1, 3):
            pcopy(n).start()

        @pl.when(turn == ALTS - 1)
        def _():
            for c in range(NZ):
                have = min(max(nfeat - c * CH, 0), CH)
                if have:
                    tho[pl.ds(c * CH, have), :] = new[at_row(c), :][:have]
            save.start()

        for n in (1, 2, 3):
            pcopy(n).wait_recv()
        fin[turn, core] = (yb[turn, 0] + yb[turn, 1]) + (yb[turn, 2] + yb[turn, 3])
        pcopy(4).start()
        pcopy(4).wait_recv()
        lab = lt[...]
        row = lax.broadcasted_iota(jnp.int32, lab.shape, 0)
        lt[...] = jnp.where(row < count, lab + (fin[turn, 0] - lab) / (1.0 + fin[turn, 1]), lab)

        for k in groups:
            for n in range(6):
                xcopy(n, k).wait_send()
        for k in range(9):
            for n in range(4):
                bcopy(n, k).wait_send()
        for d in zd:
            zcopy(d).wait_send()
            acopy(d).wait_send()
        for n in range(5):
            pcopy(n).wait_send()
        return carry

    save = pltpu.make_async_copy(tho, theta_out, sin.at[10])
    lax.fori_loop(0, ALTS, turn_body, 0)
    save.wait()
    lab_out[...] = lt[pl.ds(0, count), pl.ds(0, stars)]


def hand_over(pieces, theta, lab, theta_out, lab_out, held, held_lab, ins, outs):
    rows = [pl.ds(lo, size) for lo, size in pieces]
    into = [pltpu.make_async_copy(theta.at[r], held.at[r], ins.at[i]) for i, r in enumerate(rows)]
    away = [pltpu.make_async_copy(held.at[r], theta_out.at[r], outs.at[i]) for i, r in enumerate(rows)]
    into.append(pltpu.make_async_copy(lab, held_lab, ins.at[len(rows)]))
    away.append(pltpu.make_async_copy(held_lab, lab_out, outs.at[len(rows)]))
    for copy in into:
        copy.start()
    for done, copy in zip(into, away):
        done.wait()
        copy.start()
    for copy in away:
        copy.wait()


def per_device(flux, inv_var, coeffs, labels):
    stars, count = labels.shape
    pixels = flux.shape[1]
    nfeat = coeffs.shape[0]
    wide = -(-stars // 128) * 128
    dma = pltpu.SemaphoreType.DMA
    given = (flux, inv_var, coeffs, labels.T, *tables(count))
    scratch = [
        *[pltpu.VMEM(a.shape, a.dtype) for a in given],
        dma((11,)),
        pltpu.VMEM((nfeat, pixels), F32),
        pltpu.VMEM((ALTS + 1, F, pixels), F32),
        pltpu.VMEM((F, pixels), BF),
        pltpu.VMEM((24, wide), F32),
        pltpu.VMEM((128, 2 * F), BF),
        pltpu.VMEM((count * KL, F), BF),
        pltpu.VMEM((stars, F), BF),
        pltpu.VMEM((F, wide), BF),
        pltpu.VMEM((F, wide), BF),
        pltpu.VMEM((stars, 2 * F), BF),
        pltpu.VMEM((stars, KL), BF),
        pltpu.VMEM((wide, pixels), BF),
        pltpu.VMEM((stars, pixels), F32),
        pltpu.VMEM((wide, pixels), BF),
        pltpu.VMEM((ALTS, 2, F, pixels), F32),
        pltpu.VMEM((ALTS, 2, F, BP), F32),
        pltpu.VMEM((stars, F), F32),
        pltpu.VMEM((count // 2 * KL, 2 * BP), BF),
        pltpu.VMEM((count, stars, 128), F32),
        pltpu.VMEM((wide, 128), F32),
        pltpu.VMEM((ALTS, 8, 2, 32, 128), F32),
        pltpu.VMEM((ALTS, 8, 2, 32, 128), F32),
        pltpu.VMEM((ALTS, 8, 2, 2, 32, 128), F32),
        pltpu.VMEM((ALTS, 8, 2, 2, 32, 128), F32),
        pltpu.VMEM((ALTS, 4, 2, CH, BP), F32),
        pltpu.VMEM((ALTS, 3, 2, CH, BP), F32),
        pltpu.VMEM((ALTS, 2, 2, CH, BP), F32),
        pltpu.VMEM((ALTS, 8, 2, CH, BP), F32),
        pltpu.VMEM((ALTS, 2, 24, wide), F32),
        pltpu.VMEM((ALTS, 24, wide), F32),
        pltpu.VMEM((ALTS, NY, 24, wide), F32),
        pltpu.VMEM((ALTS, 2, 24, wide), F32),
        dma((ALTS, 6, 8)), dma((ALTS, 6, 8)),
        dma((ALTS, 15)), dma((ALTS, 15)),
        dma((ALTS, 15)), dma((ALTS, 15)),
        dma((ALTS, 4, 9)), dma((ALTS, 4, 9)),
        dma((ALTS, 5)), dma((ALTS, 5)),
    ]
    vmem = pl.BlockSpec(memory_space=pltpu.VMEM)
    theta, labt = pl.pallas_call(
        functools.partial(kernel, count, stars),
        out_shape=(
            jax.ShapeDtypeStruct((nfeat, pixels), F32),
            jax.ShapeDtypeStruct((count, stars), F32),
        ),
        in_specs=[pl.BlockSpec(memory_space=pl.ANY)] * 10,
        out_specs=(pl.BlockSpec(memory_space=pl.ANY), vmem),
        scratch_shapes=scratch,
        compiler_params=pltpu.CompilerParams(
            collective_id=0, has_side_effects=True, vmem_limit_bytes=60 * 1024 * 1024
        ),
    )(*given)
    cut = [0, 64, 128, 192, nfeat]
    pieces = [(lo, hi - lo) for lo, hi in zip(cut, cut[1:])]
    hbm = pl.BlockSpec(memory_space=pl.ANY)
    theta, labt = pl.pallas_call(
        functools.partial(hand_over, pieces),
        out_shape=(
            jax.ShapeDtypeStruct(theta.shape, F32),
            jax.ShapeDtypeStruct(labt.shape, F32),
        ),
        in_specs=[hbm, hbm],
        out_specs=(hbm, hbm),
        scratch_shapes=[
            pltpu.VMEM(theta.shape, F32),
            pltpu.VMEM(labt.shape, F32),
            dma((len(pieces) + 1,)),
            dma((len(pieces) + 1,)),
        ],
    )(theta, labt)
    return theta, labt.T


def solution(mesh):
    return jax.shard_map(
        per_device,
        mesh=mesh,
        in_specs=(P("star", "pix"), P("star", "pix"), P(None, "pix"), P("star", None)),
        out_specs=(P(None, "pix"), P("star", None)),
        check_vma=False,
    )
```
